1024 devices in a mesh: ctx: 64 (over x, z), head: 16 (over y, core).
Axes of the slice: x: 4, y: 8, z: 16, core: 2. Of those that a mesh axis runs over, the one named last changes fastest.
Arguments:
- tokens: float32 [32768, 2048], P('ctx', 'head'), may hold values from -6 to 6
- w_proj: float32 [2048, 8192], P(None, 'head'), may hold values from -0.125 to 0.125
- w_mix: float32 [2048, 144], P(None, 'head'), may hold values from -0.125 to 0.125
- conv_w: float32 [4, 6144], P(None, 'head'), may hold values from -3 to 3
- rates: float32 [16], P('head'), may hold values from 0.0001 to 0.05
- doc_start: int32 [32768], P('ctx'), may hold values 0 or 1
- norm_gain: float32 [2048], P('head'), may hold values from 0.5 to 1.5
- w_out: float32 [2048, 2048], P(None, 'head'), may hold values from -0.125 to 0.125
Outputs:
- output: float32 [32768, 2048], P('ctx', 'head')
The draws below stay inside these ranges and needn't reach their ends.
All inputs are finite; a program needn't handle non-finite values. No bound on the sum of `doc_start` on one device may be relied on, other than what follows from the above.
Results may differ from the reference program's by a relative error of at most 0.00021.
Values sent between devices are 32-bit elements; how exact they have to be, the bound alone decides.
A program may use at most 32 MiB of HBM per device.

```python
import math
import jax
import jax.numpy as jnp
from jax import lax

D = 2048
DK = 128
KERNEL = 4
LEVELS = 7
TOK_DEV = 512
HEADS = 16
NMIX = 9
TOKENS = 32768
N_CTX = 64


def place_ends(values, stream_key, least, high):
    extent = values.shape
    spot = [jax.random.randint(jax.random.fold_in(stream_key, axis), (), 0, extent[axis]) for axis in range(len(extent))]
    values = values.at[tuple(spot)].set(least)
    longest = extent.index(max(extent))
    spot[longest] = (spot[longest] + 1) % extent[longest]
    return values.at[tuple(spot)].set(high)


def block_levels(key, shape, pieces, least, high):
    level = 1.0
    for dim, blocks in pieces:
        draws = jax.random.uniform(jax.random.fold_in(jax.random.fold_in(key, 6), dim), (blocks,), jnp.float32, least / len(pieces), high / len(pieces))
        level = level * jnp.repeat(jnp.exp(draws), shape[dim] // blocks).reshape((-1,) + (1,) * (len(shape) - 1 - dim))
    return level


def normal_values(stream_key, extent, scale, limit, pieces=(), kind=jnp.bfloat16):
    drawn = scale * jax.random.normal(stream_key, extent, jnp.float32)
    if pieces:
        drawn = drawn * block_levels(stream_key, extent, pieces, -0.22, 0.18)
    return jnp.clip(drawn, -limit, limit).astype(kind)


def setup_inputs(seed: int = 0) -> dict:
    arg_keys = jax.random.split(jax.random.key(seed), 9)
    tokens = normal_values(arg_keys[0], (TOKENS, D), 1.0, 6.0, ((0, 64), (1, 16)), jnp.float32)
    w_proj = normal_values(arg_keys[1], (D, HEADS * 4 * DK), D ** -0.5, 0.125, ((1, 16),), jnp.float32)
    w_mix = normal_values(arg_keys[2], (D, HEADS * NMIX), D ** -0.5, 0.125, ((1, 16),), jnp.float32)
    conv_w = normal_values(arg_keys[3], (KERNEL, HEADS * 3 * DK), 0.5, 3.0, ((1, 16),), jnp.float32)
    rates = jnp.clip(jnp.exp(math.log(0.05) - 6.214608 * jax.random.uniform(arg_keys[4], (HEADS,), jnp.float32) ** block_levels(arg_keys[4], (HEADS,), ((0, 16),), -0.2, 0.2)), 0.0001, 0.05)
    doc_start = place_ends((jax.random.randint(arg_keys[5], (TOKENS,), 0, 1024) < 1).astype(jnp.int32), jax.random.fold_in(arg_keys[5], 1), 0, 1)
    norm_gain = jnp.clip(1.0 + 0.1 * jax.random.normal(arg_keys[6], (HEADS * DK,), jnp.float32), 0.5, 1.5)
    w_out = normal_values(arg_keys[7], (HEADS * DK, D), (HEADS * DK) ** -0.5, 0.125, ((1, 16),), jnp.float32)
    return dict(tokens=tokens, w_proj=w_proj, w_mix=w_mix, conv_w=conv_w, rates=rates, doc_start=doc_start, norm_gain=norm_gain, w_out=w_out)


def combine_pairs(first_a, first_b, second_a, second_b):
    highest = lax.Precision.HIGHEST
    new_a = jnp.einsum('nij,njk->nik', first_a, second_a, precision=highest)
    new_b = jnp.einsum('nij,njk->nik', first_b, second_a, precision=highest) + second_b
    return (new_a, new_b)

def reference(tokens, w_proj, w_mix, conv_w, rates, doc_start, norm_gain, w_out):
    highest = lax.Precision.HIGHEST
    proj_heads = w_proj.reshape(D, HEADS, 4 * DK).transpose(1, 0, 2)
    mix_heads = w_mix.reshape(D, HEADS, NMIX).transpose(1, 0, 2)
    conv_heads = conv_w.reshape(KERNEL, HEADS, 3 * DK).transpose(1, 0, 2)
    gain_heads = norm_gain.reshape(HEADS, DK)
    out_heads = w_out.reshape(HEADS, DK, D)
    resets = doc_start.astype(jnp.float32)
    nbits = N_CTX.bit_length() - 1
    identity_d = jnp.eye(DK, dtype=jnp.float32)
    block_index = jnp.arange(N_CTX, dtype=jnp.int32)

    def one_head(accum, items):
        w_head, m_head, c_head, rate, gain, o_head = items
        projected = jnp.dot(tokens, w_head, precision=highest, preferred_element_type=jnp.float32)
        mixing = jnp.dot(tokens, m_head, precision=highest, preferred_element_type=jnp.float32)
        raw_qkv = projected[:, :3 * DK]
        gate_raw = projected[:, 3 * DK:]
        padded = jnp.concatenate([jnp.zeros((KERNEL - 1, 3 * DK), jnp.float32), raw_qkv], axis=0)
        convolved = jnp.zeros((TOKENS, 3 * DK), jnp.float32)
        for step in range(KERNEL):
            convolved = convolved + c_head[step][None, :] * padded[step:step + TOKENS]
        convolved = jax.nn.silu(convolved)
        query = convolved[:, :DK]
        keys = convolved[:, DK:2 * DK]
        values = convolved[:, 2 * DK:]
        query = query / jnp.sqrt(lax.optimization_barrier(jnp.sum(query * query, axis=1, keepdims=True)) + 1e-06)
        keys = keys / jnp.sqrt(lax.optimization_barrier(jnp.sum(keys * keys, axis=1, keepdims=True)) + 1e-06)
        beta = jax.nn.sigmoid(mixing[:, 0])
        log_decay = -rate * jax.nn.softplus(mixing[:, 1]) - 20.0 * resets
        level_weight = jax.nn.softplus(mixing[:, 2:])

        def blocked(arr):
            return arr.reshape((N_CTX, TOK_DEV) + arr.shape[1:]).swapaxes(0, 1)

        def token_step(state, inputs):
            trans, memory = state
            q_t, k_t, v_t, b_t, l_t = inputs
            a_t = jnp.exp(l_t)[:, None, None]
            trans_k = jnp.einsum('nij,nj->ni', trans, k_t, precision=highest)
            trans = a_t * (trans - b_t[:, None, None] * trans_k[:, :, None] * k_t[:, None, :])
            mem_k = jnp.einsum('nij,nj->ni', memory, k_t, precision=highest)
            memory = a_t * (memory - b_t[:, None, None] * mem_k[:, :, None] * k_t[:, None, :])
            memory = memory + b_t[:, None, None] * v_t[:, :, None] * k_t[:, None, :]
            carried = jnp.einsum('nij,nj->ni', trans, q_t, precision=highest)
            local = jnp.einsum('nij,nj->ni', memory, q_t, precision=highest)
            return ((trans, memory), (carried, local))
        start = (jnp.broadcast_to(identity_d, (N_CTX, DK, DK)), jnp.zeros((N_CTX, DK, DK), jnp.float32))
        (block_a, block_b), (carried, local) = lax.scan(token_step, start, (blocked(query), blocked(keys), blocked(values), blocked(beta), blocked(log_decay)))
        carried = carried.swapaxes(0, 1)
        local = local.swapaxes(0, 1)
        weights = level_weight.reshape(N_CTX, TOK_DEV, LEVELS)
        mixed = weights[:, :, 0:1] * local
        agg_a, agg_b = (block_a, block_b)
        carry_m = jnp.broadcast_to(identity_d, (N_CTX, DK, DK))
        for level in range(nbits):
            upper = block_index >> level & 1 == 1
            source = jnp.clip((block_index >> level) - 1, 0, None)
            seg_a = jnp.where(upper[:, None, None], agg_a[source], identity_d[None])
            seg_b = jnp.where(upper[:, None, None], agg_b[source], 0.0)
            level_state = jnp.einsum('nij,njk->nik', seg_b, carry_m, precision=highest)
            carry_m = jnp.einsum('nij,njk->nik', seg_a, carry_m, precision=highest)
            mixed = mixed + weights[:, :, level + 1:level + 2] * jnp.einsum('ntk,nvk->ntv', carried, level_state, precision=highest)
            agg_a, agg_b = combine_pairs(agg_a[0::2], agg_b[0::2], agg_a[1::2], agg_b[1::2])
        mixed = mixed.reshape(TOKENS, DK)
        scale = jnp.sqrt(lax.optimization_barrier(jnp.mean(mixed * mixed, axis=1, keepdims=True)) + 1e-05)
        normed = mixed / scale * gain[None, :] * jax.nn.silu(gate_raw)
        accum = accum + jnp.dot(normed, o_head, precision=highest, preferred_element_type=jnp.float32)
        return (accum, None)
    total, unused = lax.scan(one_head, jnp.zeros((TOKENS, D), jnp.float32), (proj_heads, mix_heads, conv_heads, rates, gain_heads, out_heads))
    return total
```

```python
import jax
import jax.numpy as jnp
from jax import lax
from jax.experimental import pallas as pl
from jax.experimental.pallas import tpu as pltpu
from jax.sharding import PartitionSpec as P

F32 = jnp.float32
BF16 = jnp.bfloat16
DK = 128
CHUNK = 128
RIM = 8


def split(value):
    high = value.astype(BF16)
    return high, (value - high.astype(F32)).astype(BF16)


def left(value):
    high, low = split(value)
    return jnp.concatenate([high, low], axis=1)


def right(value):
    high, low = split(value)
    both = jnp.concatenate([high, low], axis=1)
    return jnp.concatenate([both, both], axis=0)


def product(lhs, rhs):
    out = jnp.dot(lhs, rhs, preferred_element_type=F32)
    return out[:, :DK] + out[:, DK:]


def softplus(value):
    return jnp.maximum(value, 0.0) + jnp.log1p(jnp.exp(-jnp.abs(value)))


def block_kernel(proj_ref, prior_ref, conv_ref, mix_ref, doc_ref, rate_ref,
                 carried_ref, local_ref, pair_ref, weights_ref, padded_ref):
    rows = proj_ref.shape[0]
    chunks = rows // CHUNK
    width = 3 * DK
    padded_ref[:RIM] = prior_ref[...]
    padded_ref[RIM:] = proj_ref[:, :width]
    row_ids = lax.broadcasted_iota(jnp.int32, (CHUNK, CHUNK), 0)
    col_ids = lax.broadcasted_iota(jnp.int32, (CHUNK, CHUNK), 1)
    lower = row_ids >= col_ids
    strict = row_ids > col_ids
    apart = row_ids ^ col_ids
    identity = (row_ids == col_ids).astype(F32)
    ones_lower = lower.astype(BF16)
    rate = rate_ref[0]
    mix = mix_ref[...]
    level_weights = softplus(mix)
    weights_ref[...] = level_weights
    betas = jax.nn.sigmoid(mix)

    taps = conv_ref[...]
    queries, keys, grams, cross, decays, starts, ends, tails, inverses, lowers = [], [], [], [], [], [], [], [], [], []
    weighted_keys, weighted_values = [], []
    for c in range(chunks):
        base = c * CHUNK
        total = jnp.zeros((CHUNK, width), F32)
        for step in range(4):
            first = base + RIM - 3 + step
            total = total + taps[step:step + 1] * padded_ref[first:first + CHUNK]
        total = total * jax.nn.sigmoid(total)
        q, k, v = total[:, :DK], total[:, DK:2 * DK], total[:, 2 * DK:]
        q = q * lax.rsqrt(jnp.sum(q * q, axis=1, keepdims=True) + 1e-06)
        k = k * lax.rsqrt(jnp.sum(k * k, axis=1, keepdims=True) + 1e-06)
        beta = betas[base:base + CHUNK, 0:1]
        drop = jnp.broadcast_to(-rate * level_weights[base:base + CHUNK, 1:2], (CHUNK, CHUNK))
        high, low = split(drop)
        lowest = (drop - high.astype(F32) - low.astype(F32)).astype(BF16)
        docs = jnp.broadcast_to(doc_ref[base:base + CHUNK], (CHUNK, CHUNK)).astype(BF16)
        sums = jnp.dot(ones_lower, jnp.concatenate([high, low, lowest, docs], axis=1),
                       preferred_element_type=F32)
        drift = sums[:, :CHUNK] + sums[:, CHUNK:2 * CHUNK] + sums[:, 2 * CHUNK:3 * CHUNK]
        count = sums[:, 3 * CHUNK:]
        gap = (drift - drift.T) - 20.0 * (count - count.T)
        decay = jnp.where(lower, jnp.exp(jnp.where(lower, gap, 0.0)), 0.0)
        logs = drift - 20.0 * count
        begin = jnp.exp(logs)
        key_t = right(k.T)
        both = product(left(jnp.concatenate([k, q], axis=0)), key_t)
        queries.append(q)
        keys.append(k)
        grams.append(jnp.where(strict, beta * both[:CHUNK], 0.0))
        cross.append(jnp.where(lower, both[CHUNK:], 0.0))
        decays.append(decay)
        starts.append(begin)
        ends.append(begin[CHUNK - 1:CHUNK])
        tails.append(jnp.exp((drift[CHUNK - 1:CHUNK] - drift) - 20.0 * (count[CHUNK - 1:CHUNK] - count)))
        weighted_keys.append(beta * k)
        weighted_values.append(beta * v)

    inverses = [identity - jnp.where(apart == 1, grams[c], 0.0) for c in range(chunks)]
    size = 2
    while size < CHUNK:
        member = (apart >= size) & (apart < 2 * size)
        rights = [right(inverses[c]) for c in range(chunks)]
        firsts = [product(left(jnp.where(member, grams[c], 0.0)), rights[c]) for c in range(chunks)]
        inverses = [inverses[c] - product(left(inverses[c]), right(firsts[c])) for c in range(chunks)]
        size *= 2

    state = None
    for c in range(chunks):
        base = c * CHUNK
        factor_x = product(left(inverses[c]), right(weighted_keys[c]))
        factor_y = product(left(decays[c] * inverses[c]), right(weighted_values[c]))
        right_x = right(factor_x)
        own = starts[c] * (queries[c] - product(left(cross[c]), right_x))
        near = product(left(decays[c] * cross[c]), right(factor_y))
        right_k = right(keys[c])
        ends_t = jnp.concatenate([factor_x, factor_y * tails[c]], axis=1).T
        ended = product(left(ends_t), right_k)
        trans = ends[c] * (identity - ended[:DK])
        mem = ended[DK:]
        if state is None:
            carried_ref[base:base + CHUNK] = own
            local_ref[base:base + CHUNK] = near
            state = jnp.concatenate([trans, mem], axis=0)
        else:
            own_left = left(own)
            carried_ref[base:base + CHUNK] = product(own_left, right(state[:DK].T))
            local_ref[base:base + CHUNK] = near + product(own_left, right(state[DK:].T))
            moved = product(left(state), right(trans))
            state = jnp.concatenate([moved[:DK], moved[DK:] + mem], axis=0)
    pair_ref[...] = state


def mix_kernel(carried_ref, local_ref, weights_ref, states_ref, gate_ref, gain_ref, out_ref):
    levels = states_ref.shape[0] // DK
    rows = carried_ref.shape[0]
    for base in range(0, rows, CHUNK):
        weights = weights_ref[base:base + CHUNK]
        mixed = weights[:, 2:3] * local_ref[base:base + CHUNK]
        carried = left(carried_ref[base:base + CHUNK])
        for level in range(levels):
            state = states_ref[level * DK:(level + 1) * DK].T
            mixed = mixed + weights[:, level + 3:level + 4] * product(carried, right(state))
        scale = lax.rsqrt(jnp.mean(mixed * mixed, axis=1, keepdims=True) + 1e-05)
        gate = gate_ref[base:base + CHUNK]
        out_ref[base:base + CHUNK] = mixed * scale * gain_ref[...] * (gate * jax.nn.sigmoid(gate))


def shifted(value, axis, steps):
    count = lax.axis_size(axis)
    initial, last = (max(0, -steps), min(count, count - steps))
    return lax.ppermute(value, axis, [(source, source + steps) for source in range(initial, last)])


def partner(value, axis, bit):
    mask = 2**bit
    pairs = [(source, source ^ mask) for source in range(lax.axis_size(axis))]
    return lax.ppermute(value, axis, pairs)


VMEM = pl.BlockSpec(memory_space=pltpu.VMEM)
SMEM = pl.BlockSpec(memory_space=pltpu.SMEM)


def shards(tokens, w_proj, w_mix, conv_w, rates, doc_start, norm_gain, w_out):
    high = lax.Precision.HIGH
    highest = lax.Precision.HIGHEST
    rows = tokens.shape[0]
    portion = lax.all_gather(tokens, "head", axis=1, tiled=True)
    projected = jnp.dot(portion, w_proj, precision=high, preferred_element_type=F32)
    padded_mix = jnp.pad(w_mix, ((0, 0), (0, DK - w_mix.shape[1])))
    mixing = jnp.dot(portion, padded_mix, precision=high, preferred_element_type=F32)
    prior = shifted(projected[rows - RIM:, :3 * DK], "ctx", 1)
    carried, local, pair, weights = pl.pallas_call(
        block_kernel,
        out_shape=[
            jax.ShapeDtypeStruct((rows, DK), F32),
            jax.ShapeDtypeStruct((rows, DK), F32),
            jax.ShapeDtypeStruct((2 * DK, DK), F32),
            jax.ShapeDtypeStruct((rows, DK), F32),
        ],
        in_specs=[VMEM, VMEM, VMEM, VMEM, VMEM, SMEM],
        out_specs=[VMEM] * 4,
        scratch_shapes=[pltpu.VMEM((rows + RIM, 3 * DK), F32)],
        compiler_params=pltpu.CompilerParams(vmem_limit_bytes=48 << 20),
        name="block",
    )(projected, prior, conv_w, mixing, doc_start.astype(F32)[:, None], rates)
    my_index = lax.axis_index("ctx")
    nbits = lax.axis_size("ctx").bit_length() - 1
    group_a, group_b = pair[:DK], pair[DK:]
    identity_d = jnp.eye(DK, dtype=F32)
    carry_m = identity_d
    level_states = []
    for level in range(nbits):
        other_a, other_b = partner((group_a, group_b), "ctx", level)
        upper = my_index >> level & 1 == 1
        seg_a = jnp.where(upper, other_a, identity_d)
        seg_b = jnp.where(upper, other_b, 0.0)
        first_a = jnp.where(upper, other_a, group_a)
        first_b = jnp.where(upper, other_b, group_b)
        second_a = jnp.where(upper, group_a, other_a)
        second_b = jnp.where(upper, group_b, other_b)
        group_a = jnp.dot(first_a, second_a, precision=highest, preferred_element_type=F32)
        group_b = jnp.dot(first_b, second_a, precision=highest, preferred_element_type=F32) + second_b
        level_states.append(jnp.dot(seg_b, carry_m, precision=highest, preferred_element_type=F32))
        carry_m = jnp.dot(seg_a, carry_m, precision=highest, preferred_element_type=F32)
    normed = pl.pallas_call(
        mix_kernel,
        out_shape=jax.ShapeDtypeStruct((rows, DK), F32),
        in_specs=[VMEM] * 6,
        out_specs=VMEM,
        name="mix",
    )(carried, local, weights, jnp.concatenate(level_states, axis=0), projected[:, 3 * DK:],
      norm_gain[None, :])
    every = lax.all_gather(normed, "head", axis=1, tiled=True)
    return jnp.dot(every, w_out, precision=high, preferred_element_type=F32)


def solution(mesh):
    placed = (
        P("ctx", "head"),
        P(None, "head"),
        P(None, "head"),
        P(None, "head"),
        P("head"),
        P("ctx"),
        P("head"),
        P(None, "head"),
    )
    return jax.shard_map(
        shards, mesh=mesh, in_specs=placed, out_specs=P("ctx", "head"), check_vma=False
    )
```

```python
import functools

import jax
import jax.numpy as jnp
from jax import lax
from jax.experimental import pallas as pl
from jax.experimental.pallas import tpu as pltpu
from jax.sharding import PartitionSpec as P

F32 = jnp.float32
BF16 = jnp.bfloat16
DK = 128
CHUNK = 128
RIM = 8
MESH = pl.DeviceIdType.MESH
VMEM = pl.BlockSpec(memory_space=pltpu.VMEM)
SMEM = pl.BlockSpec(memory_space=pltpu.SMEM)


def split(value):
    high = value.astype(BF16)
    return high, (value - high.astype(F32)).astype(BF16)


def left(value):
    high, low = split(value)
    return jnp.concatenate([high, low], axis=1)


def right(value):
    high, low = split(value)
    both = jnp.concatenate([high, low], axis=1)
    return jnp.concatenate([both, both], axis=0)


def product(lhs, rhs):
    out = jnp.dot(lhs, rhs, preferred_element_type=F32)
    return out[:, :DK] + out[:, DK:]


def softplus(value):
    return jnp.maximum(value, 0.0) + jnp.log1p(jnp.exp(-jnp.abs(value)))


def block_kernel(proj_ref, prior_ref, conv_ref, mix_ref, doc_ref, rate_ref,
                 carried_ref, local_ref, pair_ref, weights_ref, padded_ref):
    rows = proj_ref.shape[0]
    chunks = rows // CHUNK
    width = 3 * DK
    padded_ref[:RIM] = prior_ref[...]
    padded_ref[RIM:] = proj_ref[:, :width]
    row_ids = lax.broadcasted_iota(jnp.int32, (CHUNK, CHUNK), 0)
    col_ids = lax.broadcasted_iota(jnp.int32, (CHUNK, CHUNK), 1)
    lower = row_ids >= col_ids
    strict = row_ids > col_ids
    apart = row_ids ^ col_ids
    identity = (row_ids == col_ids).astype(F32)
    ones_lower = lower.astype(BF16)
    rate = rate_ref[0]
    mix = mix_ref[...]
    level_weights = softplus(mix)
    weights_ref[...] = level_weights
    betas = jax.nn.sigmoid(mix)

    taps = conv_ref[...]
    queries, keys, grams, cross, decays, starts, ends, tails, inverses, lowers = [], [], [], [], [], [], [], [], [], []
    weighted_keys, weighted_values = [], []
    for c in range(chunks):
        base = c * CHUNK
        total = jnp.zeros((CHUNK, width), F32)
        for step in range(4):
            first = base + RIM - 3 + step
            total = total + taps[step:step + 1] * padded_ref[first:first + CHUNK]
        total = total * jax.nn.sigmoid(total)
        q, k, v = total[:, :DK], total[:, DK:2 * DK], total[:, 2 * DK:]
        q = q * lax.rsqrt(jnp.sum(q * q, axis=1, keepdims=True) + 1e-06)
        k = k * lax.rsqrt(jnp.sum(k * k, axis=1, keepdims=True) + 1e-06)
        beta = betas[base:base + CHUNK, 0:1]
        drop = jnp.broadcast_to(-rate * level_weights[base:base + CHUNK, 1:2], (CHUNK, CHUNK))
        high, low = split(drop)
        lowest = (drop - high.astype(F32) - low.astype(F32)).astype(BF16)
        docs = jnp.broadcast_to(doc_ref[base:base + CHUNK], (CHUNK, CHUNK)).astype(BF16)
        sums = jnp.dot(ones_lower, jnp.concatenate([high, low, lowest, docs], axis=1),
                       preferred_element_type=F32)
        drift = sums[:, :CHUNK] + sums[:, CHUNK:2 * CHUNK] + sums[:, 2 * CHUNK:3 * CHUNK]
        count = sums[:, 3 * CHUNK:]
        gap = (drift - drift.T) - 20.0 * (count - count.T)
        decay = jnp.where(lower, jnp.exp(jnp.where(lower, gap, 0.0)), 0.0)
        logs = drift - 20.0 * count
        begin = jnp.exp(logs)
        key_t = right(k.T)
        both = product(left(jnp.concatenate([k, q], axis=0)), key_t)
        queries.append(q)
        keys.append(k)
        grams.append(jnp.where(strict, beta * both[:CHUNK], 0.0))
        cross.append(jnp.where(lower, both[CHUNK:], 0.0))
        decays.append(decay)
        starts.append(begin)
        ends.append(begin[CHUNK - 1:CHUNK])
        tails.append(jnp.exp((drift[CHUNK - 1:CHUNK] - drift) - 20.0 * (count[CHUNK - 1:CHUNK] - count)))
        weighted_keys.append(beta * k)
        weighted_values.append(beta * v)

    inverses = [identity - jnp.where(apart == 1, grams[c], 0.0) for c in range(chunks)]
    size = 2
    while size < CHUNK:
        member = (apart >= size) & (apart < 2 * size)
        rights = [right(inverses[c]) for c in range(chunks)]
        firsts = [product(left(jnp.where(member, grams[c], 0.0)), rights[c]) for c in range(chunks)]
        inverses = [inverses[c] - product(left(inverses[c]), right(firsts[c])) for c in range(chunks)]
        size *= 2

    state = None
    for c in range(chunks):
        base = c * CHUNK
        factor_x = product(left(inverses[c]), right(weighted_keys[c]))
        factor_y = product(left(decays[c] * inverses[c]), right(weighted_values[c]))
        right_x = right(factor_x)
        own = starts[c] * (queries[c] - product(left(cross[c]), right_x))
        near = product(left(decays[c] * cross[c]), right(factor_y))
        right_k = right(keys[c])
        ends_t = jnp.concatenate([factor_x, factor_y * tails[c]], axis=1).T
        ended = product(left(ends_t), right_k)
        trans = ends[c] * (identity - ended[:DK])
        mem = ended[DK:]
        if state is None:
            carried_ref[base:base + CHUNK] = own
            local_ref[base:base + CHUNK] = near
            state = jnp.concatenate([trans, mem], axis=0)
        else:
            own_left = left(own)
            carried_ref[base:base + CHUNK] = product(own_left, right(state[:DK].T))
            local_ref[base:base + CHUNK] = near + product(own_left, right(state[DK:].T))
            moved = product(left(state), right(trans))
            state = jnp.concatenate([moved[:DK], moved[DK:] + mem], axis=0)
    pair_ref[...] = state


def mix_kernel(carried_ref, local_ref, weights_ref, states_ref, gate_ref, gain_ref, out_ref):
    levels = states_ref.shape[0] // DK
    rows = carried_ref.shape[0]
    for base in range(0, rows, CHUNK):
        weights = weights_ref[base:base + CHUNK]
        mixed = weights[:, 2:3] * local_ref[base:base + CHUNK]
        carried = left(carried_ref[base:base + CHUNK])
        for level in range(levels):
            state = states_ref[level * DK:(level + 1) * DK].T
            mixed = mixed + weights[:, level + 3:level + 4] * product(carried, right(state))
        scale = lax.rsqrt(jnp.mean(mixed * mixed, axis=1, keepdims=True) + 1e-05)
        gate = gate_ref[base:base + CHUNK]
        out_ref[base:base + CHUNK] = mixed * scale * gain_ref[...] * (gate * jax.nn.sigmoid(gate))


PARTS = 4


def gather_kernel(x_ref, *refs, sizes):
    count = len(sizes)
    weight_refs, out_refs = refs[:count], refs[count:2 * count]
    held, store, load_sem, send_sem, recv_sem, near_send, near_recv = refs[2 * count:]
    heads = held.shape[0]
    chips = heads // 2
    half = chips // 2
    rows = x_ref.shape[0]
    part = rows // PARTS
    me = lax.axis_index("head")
    chip, core = me // 2, me % 2
    sibling = me + 1 - 2 * core
    targets = (
        lax.rem(chip + 1, chips) * 2 + core,
        lax.rem(chip + chips - 1, chips) * 2 + core,
    )
    load = pltpu.make_async_copy(weight_refs[0], store, load_sem)
    load.start()
    barrier = pltpu.get_barrier_semaphore()
    for neighbour in (*targets, sibling):
        pl.semaphore_signal(barrier, inc=1, device_id={"head": neighbour}, device_id_type=MESH)
    pl.semaphore_wait(barrier, 3)

    def slot_of(direction, hop):
        offset = chips - hop if direction == 0 else hop
        return lax.rem(chip + offset, chips) * 2 + core

    def span(index):
        return pl.ds(index * part, part)

    def ring(direction, hop, index):
        slot = slot_of(direction, hop)
        return pltpu.make_async_remote_copy(
            src_ref=held.at[slot, span(index)],
            dst_ref=held.at[slot, span(index)],
            send_sem=send_sem.at[direction, hop, index],
            recv_sem=recv_sem.at[direction, hop, index],
            device_id={"head": targets[direction]},
            device_id_type=MESH,
        )

    def first(direction, index):
        return pltpu.make_async_remote_copy(
            src_ref=x_ref.at[span(index)],
            dst_ref=held.at[me, span(index)],
            send_sem=send_sem.at[direction, 0, index],
            recv_sem=recv_sem.at[direction, 0, index],
            device_id={"head": targets[direction]},
            device_id_type=MESH,
        )

    def near(slot, offset, index, source):
        return pltpu.make_async_remote_copy(
            src_ref=source.at[span(index)],
            dst_ref=held.at[slot, span(index)],
            send_sem=near_send.at[offset, index],
            recv_sem=near_recv.at[offset, index],
            device_id={"head": sibling},
            device_id_type=MESH,
        )

    def goes(direction, hop, index):
        longest = half if (index < PARTS // 2) == (direction == 0) else half - 1
        return hop <= longest

    for index in range(PARTS):
        for direction in range(2):
            if goes(direction, 1, index):
                first(direction, index).start()
    for index in range(PARTS):
        near(me, 0, index, x_ref).start()
    held[me] = x_ref[...]
    for ref in out_refs:
        ref[...] = jnp.zeros_like(ref)
    load.wait()

    def step(hop, carry):
        for index in range(PARTS):
            for direction in range(2):
                @pl.when((hop >= 1) & goes(direction, hop, index))
                def _():
                    ring(direction, hop - 1, index).wait_recv()

                @pl.when((hop >= 1) & goes(direction, hop + 1, index))
                def _():
                    ring(direction, hop, index).start()

                @pl.when((hop >= 1) & goes(direction, hop, index))
                def _():
                    slot = slot_of(direction, hop)
                    offset = chips - hop if direction == 0 else hop
                    near(slot, offset, index, held.at[slot]).start()

        def block(which, inner):
            offset = jnp.where(which == 0, hop, chips - hop)
            offset = lax.rem(offset, chips)
            there = lax.rem(chip + offset, chips)
            for index in range(PARTS):
                other = there * 2 + 1 - core
                near(other, offset, index, held.at[other]).wait_recv()
            lhs = jnp.concatenate([held[there * 2], held[there * 2 + 1]], axis=1)
            lhs_high, lhs_low = split(lhs)
            begin = pl.multiple_of(there * 2 * DK, 2 * DK)
            for number, ref in enumerate(out_refs):
                source = store if number == 0 else weight_refs[number]
                high, low = split(source[pl.ds(begin, 2 * DK), :])
                width = high.shape[1]
                if width == DK:
                    both = jnp.concatenate([high, low], axis=1)
                    out = jnp.dot(lhs_high, both, preferred_element_type=F32)
                    ref[...] += out[:, :DK] + out[:, DK:] + jnp.dot(lhs_low, high, preferred_element_type=F32)
                else:
                    ref[...] += (
                        jnp.dot(lhs_high, high, preferred_element_type=F32)
                        + jnp.dot(lhs_high, low, preferred_element_type=F32)
                        + jnp.dot(lhs_low, high, preferred_element_type=F32)
                    )
            return inner

        lax.fori_loop(0, jnp.where((hop == 0) | (hop == half), 1, 2), block, 0)
        return carry

    lax.fori_loop(0, half + 1, step, 0)

    for index in range(PARTS):
        for direction in range(2):
            for hop in range(half):
                if goes(direction, hop + 1, index):
                    ring(direction, hop, index).wait_send()
        for offset in range(chips):
            near(me, offset, index, x_ref).wait_send()


def gather_matmul(values, weights, collective_id, name):
    rows = values.shape[0]
    heads = lax.axis_size("head")
    sizes = tuple(weight.shape[1] for weight in weights)
    half = heads // 4
    return pl.pallas_call(
        functools.partial(gather_kernel, sizes=sizes),
        out_shape=[jax.ShapeDtypeStruct((rows, size), F32) for size in sizes],
        in_specs=[VMEM, pl.BlockSpec(memory_space=pl.ANY)] + [VMEM] * (len(sizes) - 1),
        out_specs=[VMEM] * len(sizes),
        scratch_shapes=[
            pltpu.VMEM((heads, rows, DK), F32),
            pltpu.VMEM(weights[0].shape, F32),
            pltpu.SemaphoreType.DMA,
            pltpu.SemaphoreType.DMA((2, half, PARTS)),
            pltpu.SemaphoreType.DMA((2, half, PARTS)),
            pltpu.SemaphoreType.DMA((heads // 2, PARTS)),
            pltpu.SemaphoreType.DMA((heads // 2, PARTS)),
        ],
        compiler_params=pltpu.CompilerParams(
            collective_id=collective_id, has_side_effects=True, vmem_limit_bytes=48 << 20
        ),
        name=name,
    )(values, *weights)


def shifted(value, axis, steps):
    count = lax.axis_size(axis)
    initial, last = (max(0, -steps), min(count, count - steps))
    return lax.ppermute(value, axis, [(source, source + steps) for source in range(initial, last)])


def partner(value, axis, bit):
    mask = 2**bit
    pairs = [(source, source ^ mask) for source in range(lax.axis_size(axis))]
    return lax.ppermute(value, axis, pairs)


def shards(tokens, w_proj, w_mix, conv_w, rates, doc_start, norm_gain, w_out):
    highest = lax.Precision.HIGHEST
    rows = tokens.shape[0]
    projected, mixing = gather_matmul(tokens, [w_proj, w_mix], 0, "project")
    prior = shifted(projected[rows - RIM:, :3 * DK], "ctx", 1)
    carried, local, pair, weights = pl.pallas_call(
        block_kernel,
        out_shape=[
            jax.ShapeDtypeStruct((rows, DK), F32),
            jax.ShapeDtypeStruct((rows, DK), F32),
            jax.ShapeDtypeStruct((2 * DK, DK), F32),
            jax.ShapeDtypeStruct(mixing.shape, F32),
        ],
        in_specs=[VMEM, VMEM, VMEM, VMEM, VMEM, SMEM],
        out_specs=[VMEM] * 4,
        scratch_shapes=[pltpu.VMEM((rows + RIM, 3 * DK), F32)],
        compiler_params=pltpu.CompilerParams(vmem_limit_bytes=48 << 20),
        name="block",
    )(projected, prior, conv_w, mixing, doc_start.astype(F32)[:, None], rates)
    my_index = lax.axis_index("ctx")
    nbits = lax.axis_size("ctx").bit_length() - 1
    group_a, group_b = pair[:DK], pair[DK:]
    identity_d = jnp.eye(DK, dtype=F32)
    carry_m = identity_d
    level_states = []
    for level in range(nbits):
        other_a, other_b = partner((group_a, group_b), "ctx", level)
        upper = my_index >> level & 1 == 1
        seg_a = jnp.where(upper, other_a, identity_d)
        seg_b = jnp.where(upper, other_b, 0.0)
        first_a = jnp.where(upper, other_a, group_a)
        first_b = jnp.where(upper, other_b, group_b)
        second_a = jnp.where(upper, group_a, other_a)
        second_b = jnp.where(upper, group_b, other_b)
        group_a = jnp.dot(first_a, second_a, precision=highest, preferred_element_type=F32)
        group_b = jnp.dot(first_b, second_a, precision=highest, preferred_element_type=F32) + second_b
        level_states.append(jnp.dot(seg_b, carry_m, precision=highest, preferred_element_type=F32))
        carry_m = jnp.dot(seg_a, carry_m, precision=highest, preferred_element_type=F32)
    normed = pl.pallas_call(
        mix_kernel,
        out_shape=jax.ShapeDtypeStruct((rows, DK), F32),
        in_specs=[VMEM] * 6,
        out_specs=VMEM,
        name="mix",
    )(carried, local, weights, jnp.concatenate(level_states, axis=0), projected[:, 3 * DK:],
      norm_gain[None, :])
    return gather_matmul(normed, [w_out], 1, "combine")[0]


def solution(mesh):
    placed = (
        P("ctx", "head"),
        P(None, "head"),
        P(None, "head"),
        P(None, "head"),
        P("head"),
        P("ctx"),
        P("head"),
        P(None, "head"),
    )
    return jax.shard_map(
        shards, mesh=mesh, in_specs=placed, out_specs=P("ctx", "head"), check_vma=False
    )
```

```python
import functools

import jax
import jax.numpy as jnp
from jax import lax
from jax.experimental import pallas as pl
from jax.experimental.pallas import tpu as pltpu
from jax.sharding import PartitionSpec as P

F32 = jnp.float32
BF16 = jnp.bfloat16
DK = 128
CHUNK = 128
RIM = 8
MESH = pl.DeviceIdType.MESH
VMEM = pl.BlockSpec(memory_space=pltpu.VMEM)
SMEM = pl.BlockSpec(memory_space=pltpu.SMEM)


def split(value):
    high = value.astype(BF16)
    return high, (value - high.astype(F32)).astype(BF16)


def left(value):
    high, low = split(value)
    return jnp.concatenate([high, low], axis=1)


def right(value):
    high, low = split(value)
    both = jnp.concatenate([high, low], axis=1)
    return jnp.concatenate([both, both], axis=0)


def product(lhs, rhs):
    out = jnp.dot(lhs, rhs, preferred_element_type=F32)
    return out[:, :DK] + out[:, DK:]


def softplus(value):
    return jnp.maximum(value, 0.0) + jnp.log1p(jnp.exp(-jnp.abs(value)))


def block_kernel(proj_ref, prior_ref, conv_ref, mix_ref, doc_ref, rate_ref,
                 carried_ref, local_ref, pair_ref, weights_ref, padded_ref):
    rows = proj_ref.shape[0]
    chunks = rows // CHUNK
    width = 3 * DK
    padded_ref[:RIM] = prior_ref[...]
    padded_ref[RIM:] = proj_ref[:, :width]
    row_ids = lax.broadcasted_iota(jnp.int32, (CHUNK, CHUNK), 0)
    col_ids = lax.broadcasted_iota(jnp.int32, (CHUNK, CHUNK), 1)
    lower = row_ids >= col_ids
    strict = row_ids > col_ids
    apart = row_ids ^ col_ids
    identity = (row_ids == col_ids).astype(F32)
    ones_lower = lower.astype(BF16)
    rate = rate_ref[0]
    mix = mix_ref[...]
    level_weights = softplus(mix)
    weights_ref[...] = level_weights
    betas = jax.nn.sigmoid(mix)

    taps = conv_ref[...]
    queries, keys, grams, cross, decays, starts, ends, tails, inverses, lowers = [], [], [], [], [], [], [], [], [], []
    weighted_keys, weighted_values = [], []
    for c in range(chunks):
        base = c * CHUNK
        total = jnp.zeros((CHUNK, width), F32)
        for step in range(4):
            first = base + RIM - 3 + step
            total = total + taps[step:step + 1] * padded_ref[first:first + CHUNK]
        total = total * jax.nn.sigmoid(total)
        q, k, v = total[:, :DK], total[:, DK:2 * DK], total[:, 2 * DK:]
        q = q * lax.rsqrt(jnp.sum(q * q, axis=1, keepdims=True) + 1e-06)
        k = k * lax.rsqrt(jnp.sum(k * k, axis=1, keepdims=True) + 1e-06)
        beta = betas[base:base + CHUNK, 0:1]
        drop = jnp.broadcast_to(-rate * level_weights[base:base + CHUNK, 1:2], (CHUNK, CHUNK))
        high, low = split(drop)
        lowest = (drop - high.astype(F32) - low.astype(F32)).astype(BF16)
        docs = jnp.broadcast_to(doc_ref[base:base + CHUNK], (CHUNK, CHUNK)).astype(BF16)
        sums = jnp.dot(ones_lower, jnp.concatenate([high, low, lowest, docs], axis=1),
                       preferred_element_type=F32)
        drift = sums[:, :CHUNK] + sums[:, CHUNK:2 * CHUNK] + sums[:, 2 * CHUNK:3 * CHUNK]
        count = sums[:, 3 * CHUNK:]
        gap = (drift - drift.T) - 20.0 * (count - count.T)
        decay = jnp.where(lower, jnp.exp(jnp.where(lower, gap, 0.0)), 0.0)
        logs = drift - 20.0 * count
        begin = jnp.exp(logs)
        key_t = right(k.T)
        both = product(left(jnp.concatenate([k, q], axis=0)), key_t)
        queries.append(q)
        keys.append(k)
        grams.append(jnp.where(strict, beta * both[:CHUNK], 0.0))
        cross.append(jnp.where(lower, both[CHUNK:], 0.0))
        decays.append(decay)
        starts.append(begin)
        ends.append(begin[CHUNK - 1:CHUNK])
        tails.append(jnp.exp((drift[CHUNK - 1:CHUNK] - drift) - 20.0 * (count[CHUNK - 1:CHUNK] - count)))
        weighted_keys.append(beta * k)
        weighted_values.append(beta * v)

    inverses = [identity - jnp.where(apart == 1, grams[c], 0.0) for c in range(chunks)]
    size = 2
    while size < CHUNK:
        member = (apart >= size) & (apart < 2 * size)
        rights = [right(inverses[c]) for c in range(chunks)]
        firsts = [product(left(jnp.where(member, grams[c], 0.0)), rights[c]) for c in range(chunks)]
        inverses = [inverses[c] - product(left(inverses[c]), right(firsts[c])) for c in range(chunks)]
        size *= 2

    state = None
    for c in range(chunks):
        base = c * CHUNK
        factor_x = product(left(inverses[c]), right(weighted_keys[c]))
        factor_y = product(left(decays[c] * inverses[c]), right(weighted_values[c]))
        right_x = right(factor_x)
        own = starts[c] * (queries[c] - product(left(cross[c]), right_x))
        near = product(left(decays[c] * cross[c]), right(factor_y))
        right_k = right(keys[c])
        ends_t = jnp.concatenate([factor_x, factor_y * tails[c]], axis=1).T
        ended = product(left(ends_t), right_k)
        trans = ends[c] * (identity - ended[:DK])
        mem = ended[DK:]
        if state is None:
            carried_ref[base:base + CHUNK] = own
            local_ref[base:base + CHUNK] = near
            state = jnp.concatenate([trans, mem], axis=0)
        else:
            own_left = left(own)
            carried_ref[base:base + CHUNK] = product(own_left, right(state[:DK].T))
            local_ref[base:base + CHUNK] = near + product(own_left, right(state[DK:].T))
            moved = product(left(state), right(trans))
            state = jnp.concatenate([moved[:DK], moved[DK:] + mem], axis=0)
    pair_ref[...] = state


PARTS = 4


def gather_kernel(x_ref, *refs, sizes):
    count = len(sizes)
    weight_refs, out_refs = refs[:count], refs[count:2 * count]
    held, store, load_sem, send_sem, recv_sem, near_send, near_recv = refs[2 * count:]
    heads = held.shape[0]
    chips = heads // 2
    half = chips // 2
    rows = x_ref.shape[0]
    part = rows // PARTS
    me = lax.axis_index("head")
    chip, core = me // 2, me % 2
    sibling = me + 1 - 2 * core
    targets = (
        lax.rem(chip + 1, chips) * 2 + core,
        lax.rem(chip + chips - 1, chips) * 2 + core,
    )
    load = pltpu.make_async_copy(weight_refs[0], store, load_sem)
    load.start()
    barrier = pltpu.get_barrier_semaphore()
    for neighbour in (*targets, sibling):
        pl.semaphore_signal(barrier, inc=1, device_id={"head": neighbour}, device_id_type=MESH)
    pl.semaphore_wait(barrier, 3)

    def slot_of(direction, hop):
        offset = chips - hop if direction == 0 else hop
        return lax.rem(chip + offset, chips) * 2 + core

    def span(index):
        return pl.ds(index * part, part)

    def ring(direction, hop, index):
        slot = slot_of(direction, hop)
        return pltpu.make_async_remote_copy(
            src_ref=held.at[slot, span(index)],
            dst_ref=held.at[slot, span(index)],
            send_sem=send_sem.at[direction, hop, index],
            recv_sem=recv_sem.at[direction, hop, index],
            device_id={"head": targets[direction]},
            device_id_type=MESH,
        )

    def first(direction, index):
        return pltpu.make_async_remote_copy(
            src_ref=x_ref.at[span(index)],
            dst_ref=held.at[me, span(index)],
            send_sem=send_sem.at[direction, 0, index],
            recv_sem=recv_sem.at[direction, 0, index],
            device_id={"head": targets[direction]},
            device_id_type=MESH,
        )

    def near(slot, offset, index, source):
        return pltpu.make_async_remote_copy(
            src_ref=source.at[span(index)],
            dst_ref=held.at[slot, span(index)],
            send_sem=near_send.at[offset, index],
            recv_sem=near_recv.at[offset, index],
            device_id={"head": sibling},
            device_id_type=MESH,
        )

    def goes(direction, hop, index):
        longest = half if (index < PARTS // 2) == (direction == 0) else half - 1
        return hop <= longest

    for index in range(PARTS):
        for direction in range(2):
            if goes(direction, 1, index):
                first(direction, index).start()
    for index in range(PARTS):
        near(me, 0, index, x_ref).start()
    held[me] = x_ref[...]
    for ref in out_refs:
        ref[...] = jnp.zeros_like(ref)
    load.wait()

    def step(hop, carry):
        for index in range(PARTS):
            for direction in range(2):
                @pl.when((hop >= 1) & goes(direction, hop, index))
                def _():
                    ring(direction, hop - 1, index).wait_recv()

                @pl.when((hop >= 1) & goes(direction, hop + 1, index))
                def _():
                    ring(direction, hop, index).start()

                @pl.when((hop >= 1) & goes(direction, hop, index))
                def _():
                    slot = slot_of(direction, hop)
                    offset = chips - hop if direction == 0 else hop
                    near(slot, offset, index, held.at[slot]).start()

        def block(which, inner):
            offset = jnp.where(which == 0, hop, chips - hop)
            offset = lax.rem(offset, chips)
            there = lax.rem(chip + offset, chips)
            for index in range(PARTS):
                other = there * 2 + 1 - core
                near(other, offset, index, held.at[other]).wait_recv()
            lhs = jnp.concatenate([held[there * 2], held[there * 2 + 1]], axis=1)
            lhs_high, lhs_low = split(lhs)
            begin = pl.multiple_of(there * 2 * DK, 2 * DK)
            for number, ref in enumerate(out_refs):
                source = store if number == 0 else weight_refs[number]
                high, low = split(source[pl.ds(begin, 2 * DK), :])
                width = high.shape[1]
                if width == DK:
                    both = jnp.concatenate([high, low], axis=1)
                    out = jnp.dot(lhs_high, both, preferred_element_type=F32)
                    ref[...] += out[:, :DK] + out[:, DK:] + jnp.dot(lhs_low, high, preferred_element_type=F32)
                else:
                    ref[...] += (
                        jnp.dot(lhs_high, high, preferred_element_type=F32)
                        + jnp.dot(lhs_high, low, preferred_element_type=F32)
                        + jnp.dot(lhs_low, high, preferred_element_type=F32)
                    )
            return inner

        lax.fori_loop(0, jnp.where((hop == 0) | (hop == half), 1, 2), block, 0)
        return carry

    lax.fori_loop(0, half + 1, step, 0)

    for index in range(PARTS):
        for direction in range(2):
            for hop in range(half):
                if goes(direction, hop + 1, index):
                    ring(direction, hop, index).wait_send()
        for offset in range(chips):
            near(me, offset, index, x_ref).wait_send()


def gather_matmul(values, weights, collective_id, name):
    rows = values.shape[0]
    heads = lax.axis_size("head")
    sizes = tuple(weight.shape[1] for weight in weights)
    half = heads // 4
    return pl.pallas_call(
        functools.partial(gather_kernel, sizes=sizes),
        out_shape=[jax.ShapeDtypeStruct((rows, size), F32) for size in sizes],
        in_specs=[VMEM, pl.BlockSpec(memory_space=pl.ANY)] + [VMEM] * (len(sizes) - 1),
        out_specs=[VMEM] * len(sizes),
        scratch_shapes=[
            pltpu.VMEM((heads, rows, DK), F32),
            pltpu.VMEM(weights[0].shape, F32),
            pltpu.SemaphoreType.DMA,
            pltpu.SemaphoreType.DMA((2, half, PARTS)),
            pltpu.SemaphoreType.DMA((2, half, PARTS)),
            pltpu.SemaphoreType.DMA((heads // 2, PARTS)),
            pltpu.SemaphoreType.DMA((heads // 2, PARTS)),
        ],
        compiler_params=pltpu.CompilerParams(
            collective_id=collective_id, has_side_effects=True, vmem_limit_bytes=48 << 20
        ),
        name=name,
    )(values, *weights)


NZ = 16
RING_PARTS = 4


class Ring:
    def __init__(self, place, n, targets, source, held, send_sem, recv_sem, parts=RING_PARTS):
        self.place, self.n, self.targets, self.source, self.held = place, n, targets, source, held
        self.send_sem, self.recv_sem, self.parts = send_sem, recv_sem, parts
        self.half = n // 2
        self.part = source.shape[0] // parts

    def goes(self, direction, hop, index):
        longest = self.half if (index < self.parts // 2) == (direction == 0) else self.half - 1
        return hop <= longest

    def copy(self, direction, hop, index, first=False):
        span = pl.ds(index * self.part, self.part)
        offset = self.n - hop if direction == 0 else hop
        slot = self.place if first else lax.rem(self.place + offset, self.n)
        source = self.source if first else self.held.at[slot]
        return pltpu.make_async_remote_copy(
            src_ref=source.at[span],
            dst_ref=self.held.at[slot, span],
            send_sem=self.send_sem.at[direction, hop, index],
            recv_sem=self.recv_sem.at[direction, hop, index],
            device_id=self.targets[direction],
            device_id_type=MESH,
        )

    def begin(self):
        for index in range(self.parts):
            for direction in range(2):
                if self.goes(direction, 1, index):
                    self.copy(direction, 0, index, True).start()
        self.held[self.place] = self.source[...]

    def arrive(self, hop):
        for index in range(self.parts):
            for direction in range(2):
                @pl.when(self.goes(direction, hop, index))
                def _():
                    self.copy(direction, hop - 1, index).wait_recv()

                @pl.when(self.goes(direction, hop + 1, index))
                def _():
                    self.copy(direction, hop, index).start()

    def run(self):
        def step(hop, carry):
            self.arrive(hop)
            return carry

        lax.fori_loop(1, self.half + 1, step, 0)

    def end(self):
        for index in range(self.parts):
            for direction in range(2):
                for hop in range(self.half):
                    if self.goes(direction, hop + 1, index):
                        self.copy(direction, hop, index, True).wait_send()


def join(first, second):
    moved = product(left(first), right(second[:DK]))
    return jnp.concatenate([moved[:DK], moved[DK:] + second[DK:]], axis=0)


def reduce_ring(held, tree, count, last):
    nodes = [held[index] for index in range(count)]
    level = 0
    while len(nodes) > (1 if last else 2):
        nodes = [join(nodes[2 * index], nodes[2 * index + 1]) for index in range(len(nodes) // 2)]
        if len(nodes) > 1:
            for index, node in enumerate(nodes):
                tree[level, index] = node
        level += 1
    return nodes[0]


def level_states(held, tree, count, place, carry, neutral):
    states = []
    for level in range(count.bit_length() - 1):
        upper = (place >> level) & 1 == 1
        index = jnp.maximum((place >> level) - 1, 0)
        node = held[index] if level == 0 else tree[level - 1, index]
        moved = product(left(jnp.where(upper, node, neutral)), right(carry))
        carry = moved[:DK]
        states.append(moved[DK:])
    return states, carry


def context_kernel(pair_ref, carried_ref, local_ref, weights_ref, gate_ref, gain_ref, out_ref,
                   held_z, tree_z, held_x, tree_x, group_ref, mixed_ref,
                   send_z, recv_z, send_x, recv_x):
    count_z, count_x = held_z.shape[0], held_x.shape[0]
    rows = carried_ref.shape[0]
    me = lax.axis_index("ctx")
    place_x, place_z = me // count_z, lax.rem(me, count_z)
    targets_z = [
        {"ctx": place_x * count_z + lax.rem(place_z + offset, count_z)} for offset in (1, count_z - 1)
    ]
    targets_x = [
        {"ctx": lax.rem(place_x + offset, count_x) * count_z + place_z} for offset in (1, count_x - 1)
    ]
    barrier = pltpu.get_barrier_semaphore()
    for neighbour in targets_z + targets_x:
        pl.semaphore_signal(barrier, inc=1, device_id=neighbour, device_id_type=MESH)
    pl.semaphore_wait(barrier, 4)

    ring_z = Ring(place_z, count_z, targets_z, pair_ref, held_z, send_z, recv_z)
    ring_x = Ring(place_x, count_x, targets_x, group_ref, held_x, send_x, recv_x)
    ring_z.begin()
    ring_z.run()
    group_ref[...] = reduce_ring(held_z, tree_z, count_z, True)
    ring_x.begin()

    row_ids = lax.broadcasted_iota(jnp.int32, (2 * DK, DK), 0)
    col_ids = lax.broadcasted_iota(jnp.int32, (2 * DK, DK), 1)
    neutral = (row_ids == col_ids).astype(F32)
    states, carry = level_states(held_z, tree_z, count_z, place_z, neutral[:DK], neutral)
    done = len(states)

    def mix(base, total, states, first):
        carried = left(carried_ref[base:base + CHUNK])
        for number, state in enumerate(states):
            column = first + number
            weight = weights_ref[base:base + CHUNK, column:column + 1]
            total = total + weight * product(carried, state)
        return total

    turned = [right(state.T) for state in states]
    for base in range(0, rows, CHUNK):
        start = weights_ref[base:base + CHUNK, 2:3] * local_ref[base:base + CHUNK]
        mixed_ref[base:base + CHUNK] = mix(base, start, turned, 3)
    ring_x.run()
    reduce_ring(held_x, tree_x, count_x, False)
    states, carry = level_states(held_x, tree_x, count_x, place_x, carry, neutral)
    turned = [right(state.T) for state in states]
    for base in range(0, rows, CHUNK):
        mixed = mix(base, mixed_ref[base:base + CHUNK], turned, 3 + done)
        scale = lax.rsqrt(jnp.mean(mixed * mixed, axis=1, keepdims=True) + 1e-05)
        gate = gate_ref[base:base + CHUNK]
        out_ref[base:base + CHUNK] = mixed * scale * gain_ref[...] * (gate * jax.nn.sigmoid(gate))
    ring_z.end()
    ring_x.end()


def across_context(pair, carried, local, weights, projected, gain):
    rows = carried.shape[0]
    count = lax.axis_size("ctx")
    count_z = min(NZ, count)
    count_x = count // count_z
    return pl.pallas_call(
        context_kernel,
        out_shape=jax.ShapeDtypeStruct((rows, DK), F32),
        grid=(1,),
        in_specs=[VMEM] * 4 + [pl.BlockSpec((rows, DK), lambda step: (0, 3)), VMEM],
        out_specs=VMEM,
        scratch_shapes=[
            pltpu.VMEM((count_z, 2 * DK, DK), F32),
            pltpu.VMEM((count_z.bit_length() - 2, count_z // 2, 2 * DK, DK), F32),
            pltpu.VMEM((count_x, 2 * DK, DK), F32),
            pltpu.VMEM((max(count_x.bit_length() - 2, 1), count_x // 2, 2 * DK, DK), F32),
            pltpu.VMEM((2 * DK, DK), F32),
            pltpu.VMEM((rows, DK), F32),
        ] + [pltpu.SemaphoreType.DMA((2, count_z // 2, RING_PARTS))] * 2
          + [pltpu.SemaphoreType.DMA((2, count_x // 2, RING_PARTS))] * 2,
        compiler_params=pltpu.CompilerParams(
            collective_id=2, has_side_effects=True, vmem_limit_bytes=48 << 20
        ),
        name="context",
    )(pair, carried, local, weights, projected, gain)


def shifted(value, axis, steps):
    count = lax.axis_size(axis)
    initial, last = (max(0, -steps), min(count, count - steps))
    return lax.ppermute(value, axis, [(source, source + steps) for source in range(initial, last)])


def shards(tokens, w_proj, w_mix, conv_w, rates, doc_start, norm_gain, w_out):
    rows = tokens.shape[0]
    projected, mixing = gather_matmul(tokens, [w_proj, w_mix], 0, "project")
    prior = shifted(projected[rows - RIM:, :3 * DK], "ctx", 1)
    carried, local, pair, weights = pl.pallas_call(
        block_kernel,
        out_shape=[
            jax.ShapeDtypeStruct((rows, DK), F32),
            jax.ShapeDtypeStruct((rows, DK), F32),
            jax.ShapeDtypeStruct((2 * DK, DK), F32),
            jax.ShapeDtypeStruct(mixing.shape, F32),
        ],
        in_specs=[VMEM, VMEM, VMEM, VMEM, VMEM, SMEM],
        out_specs=[VMEM] * 4,
        scratch_shapes=[pltpu.VMEM((rows + RIM, 3 * DK), F32)],
        compiler_params=pltpu.CompilerParams(vmem_limit_bytes=48 << 20),
        name="block",
    )(projected, prior, conv_w, mixing, doc_start.astype(F32)[:, None], rates)
    normed = across_context(pair, carried, local, weights, projected, norm_gain[None, :])
    return gather_matmul(normed, [w_out], 1, "combine")[0]


def solution(mesh):
    placed = (
        P("ctx", "head"),
        P(None, "head"),
        P(None, "head"),
        P(None, "head"),
        P("head"),
        P("ctx"),
        P("head"),
        P(None, "head"),
    )
    return jax.shard_map(
        shards, mesh=mesh, in_specs=placed, out_specs=P("ctx", "head"), check_vma=False
    )
```

```python
import jax
import jax.numpy as jnp
from jax import lax
from jax.experimental import pallas as pl
from jax.experimental.pallas import tpu as pltpu
from jax.sharding import PartitionSpec as P

F32 = jnp.float32
BF16 = jnp.bfloat16
DK = 128
CHUNK = 128
RIM = 8
NZ = 16
PARTS = 4
MESH = pl.DeviceIdType.MESH
VMEM = pl.BlockSpec(memory_space=pltpu.VMEM)
SMEM = pl.BlockSpec(memory_space=pltpu.SMEM)
ANY = pl.BlockSpec(memory_space=pl.ANY)


def split(value):
    high = value.astype(BF16)
    return high, (value - high.astype(F32)).astype(BF16)


def left(value):
    high, low = split(value)
    return jnp.concatenate([high, low], axis=1)


def right(value):
    high, low = split(value)
    both = jnp.concatenate([high, low], axis=1)
    return jnp.concatenate([both, both], axis=0)


def product(lhs, rhs):
    out = jnp.dot(lhs, rhs, preferred_element_type=F32)
    return out[:, :DK] + out[:, DK:]


def softplus(value):
    return jnp.maximum(value, 0.0) + jnp.log1p(jnp.exp(-jnp.abs(value)))


def join(first, second):
    moved = product(left(first), right(second[:DK]))
    return jnp.concatenate([moved[:DK], moved[DK:] + second[DK:]], axis=0)


class Ring:
    def __init__(self, place, n, targets, source, held, send_sem, recv_sem, stride=1, phase=0, pass_on=None):
        self.place, self.n, self.targets, self.source, self.held = place, n, targets, source, held
        self.send_sem, self.recv_sem, self.stride, self.phase = send_sem, recv_sem, stride, phase
        self.pass_on = pass_on
        self.half = n // 2
        self.part = source.shape[0] // PARTS

    def slot(self, place):
        return place * self.stride + self.phase

    def span(self, index):
        return pl.ds(index * self.part, self.part)

    def goes(self, direction, hop, index):
        longest = self.half if (index < PARTS // 2) == (direction == 0) else self.half - 1
        return hop <= longest

    def offset(self, direction, hop):
        return lax.rem(self.n - hop if direction == 0 else hop + 0, self.n)

    def copy(self, direction, hop, index, first=False):
        slot = self.slot(self.place if first else lax.rem(self.place + self.offset(direction, hop), self.n))
        source = self.source if first else self.held.at[slot]
        return pltpu.make_async_remote_copy(
            src_ref=source.at[self.span(index)],
            dst_ref=self.held.at[slot, self.span(index)],
            send_sem=self.send_sem.at[direction, hop, index],
            recv_sem=self.recv_sem.at[direction, hop, index],
            device_id=self.targets[direction],
            device_id_type=MESH,
        )

    def begin(self, index):
        for direction in range(2):
            if self.goes(direction, 1, index):
                self.copy(direction, 0, index, True).start()
        if self.pass_on is not None:
            self.pass_on(self.slot(self.place), 0, index, self.source).start()

    def arrive(self, hop, guard=True):
        for index in range(PARTS):
            for direction in range(2):
                here = guard & self.goes(direction, hop, index)

                @pl.when(here)
                def _():
                    self.copy(direction, hop - 1, index).wait_recv()

                @pl.when(guard & self.goes(direction, hop + 1, index))
                def _():
                    self.copy(direction, hop, index).start()

                if self.pass_on is not None:
                    @pl.when(here)
                    def _():
                        offset = self.offset(direction, hop)
                        slot = self.slot(lax.rem(self.place + offset, self.n))
                        self.pass_on(slot, offset, index, self.held.at[slot]).start()

    def run(self, first=1):
        def step(hop, carry):
            self.arrive(hop)
            return carry

        lax.fori_loop(first, self.half + 1, step, 0)

    def end(self):
        for index in range(PARTS):
            for direction in range(2):
                for hop in range(self.half):
                    if self.goes(direction, hop + 1, index):
                        self.copy(direction, hop, index, True).wait_send()
            if self.pass_on is not None:
                for offset in range(self.n):
                    self.pass_on(self.slot(self.place), offset, index, self.source).wait_send()


def multiply_arrivals(ring, multiply):
    def step(hop, carry):
        ring.arrive(hop, hop >= 1)

        def block(which, inner):
            offset = lax.rem(jnp.where(which == 0, hop, ring.n - hop), ring.n)
            there = lax.rem(ring.place + offset, ring.n)
            for index in range(PARTS):
                other = there * 2 + 1 - ring.phase
                ring.pass_on(other, offset, index, ring.held.at[other]).wait_recv()
            lhs = jnp.concatenate([ring.held[there * 2], ring.held[there * 2 + 1]], axis=1)
            multiply(split(lhs), pl.multiple_of(there * 2 * DK, 2 * DK))
            return inner

        lax.fori_loop(0, jnp.where((hop == 0) | (hop == ring.half), 1, 2), block, 0)
        return carry

    lax.fori_loop(0, ring.half + 1, step, 0)


def reduce_ring(held, tree, count, last):
    nodes = [held[index] for index in range(count)]
    level = 0
    while len(nodes) > (1 if last else 2):
        nodes = [join(nodes[2 * index], nodes[2 * index + 1]) for index in range(len(nodes) // 2)]
        if len(nodes) > 1:
            for index, node in enumerate(nodes):
                tree[level, index] = node
        level += 1
    return nodes[0]


def level_states(held, tree, count, place, carry, neutral):
    states = []
    for level in range(count.bit_length() - 1):
        upper = (place >> level) & 1 == 1
        index = jnp.maximum((place >> level) - 1, 0)
        node = held[index] if level == 0 else tree[level - 1, index]
        moved = product(left(jnp.where(upper, node, neutral)), right(carry))
        carry = moved[:DK]
        states.append(moved[DK:])
    return states, carry


def layer(tokens_ref, w_proj_ref, w_mix_ref, conv_ref, rate_ref, doc_ref, gain_ref, w_out_ref, out_ref,
          held_in, held_out, w_proj, w_out, raw_ref, mixing_ref, padded_ref, prior_ref,
          pair_ref, held_z, tree_z, group_ref, held_x, tree_x, local_ref, carried_ref, normed_ref,
          load_sem, rim_sem, send_y, recv_y, near_send, near_recv,
          send_z, recv_z, send_x, recv_x):
    rows = tokens_ref.shape[0]
    chunks = rows // CHUNK
    width = 3 * DK
    heads = held_in.shape[0]
    chips = heads // 2
    count_z, count_x = held_z.shape[0], held_x.shape[0]
    blocks = count_z * count_x

    head = lax.axis_index("head")
    chip, core = head // 2, lax.rem(head, 2)
    me = lax.axis_index("ctx")
    place_x, place_z = me // count_z, lax.rem(me, count_z)
    targets_y = [{"head": lax.rem(chip + offset, chips) * 2 + core} for offset in (1, chips - 1)]
    sibling = {"head": head + 1 - 2 * core}
    targets_z = [
        {"ctx": place_x * count_z + lax.rem(place_z + offset, count_z)} for offset in (1, count_z - 1)
    ]
    targets_x = [
        {"ctx": lax.rem(place_x + offset, count_x) * count_z + place_z} for offset in (1, count_x - 1)
    ]
    after, before = {"ctx": lax.rem(me + 1, blocks)}, {"ctx": lax.rem(me + blocks - 1, blocks)}

    loads = [
        pltpu.make_async_copy(w_proj_ref, w_proj, load_sem.at[0]),
        pltpu.make_async_copy(w_out_ref, w_out, load_sem.at[1]),
    ]
    for load in loads:
        load.start()
    barrier = pltpu.get_barrier_semaphore()
    partners = targets_y + [sibling] + targets_z + targets_x + [after, before]
    for partner in partners:
        pl.semaphore_signal(barrier, inc=1, device_id=partner, device_id_type=MESH)
    pl.semaphore_wait(barrier, len(partners))

    def near(held, number):
        def copy(slot, offset, index, source):
            part = rows // PARTS
            span = pl.ds(index * part, part)
            return pltpu.make_async_remote_copy(
                src_ref=source.at[span],
                dst_ref=held.at[slot, span],
                send_sem=near_send.at[number, offset, index],
                recv_sem=near_recv.at[number, offset, index],
                device_id=sibling,
                device_id_type=MESH,
            )

        return copy

    ring_in = Ring(chip, chips, targets_y, tokens_ref, held_in, send_y.at[0], recv_y.at[0], 2, core, near(held_in, 0))
    ring_out = Ring(chip, chips, targets_y, normed_ref, held_out, send_y.at[1], recv_y.at[1], 2, core, near(held_out, 1))
    ring_z = Ring(place_z, count_z, targets_z, pair_ref, held_z, send_z, recv_z)
    ring_x = Ring(place_x, count_x, targets_x, group_ref, held_x, send_x, recv_x)

    for index in range(PARTS):
        ring_in.begin(index)
    held_in[head] = tokens_ref[...]
    raw_ref[...] = jnp.zeros_like(raw_ref)
    mixing_ref[...] = jnp.zeros_like(mixing_ref)
    out_ref[...] = jnp.zeros_like(out_ref)
    for load in loads:
        load.wait()

    def project(lhs, begin):
        high, low = split(w_proj[pl.ds(begin, 2 * DK), :])
        raw_ref[...] += (
            jnp.dot(lhs[0], high, preferred_element_type=F32)
            + jnp.dot(lhs[0], low, preferred_element_type=F32)
            + jnp.dot(lhs[1], high, preferred_element_type=F32)
        )
        high, low = split(w_mix_ref[:, pl.ds(begin, 2 * DK)])
        dims = (((1,), (1,)), ((), ()))
        mixing_ref[...] += (
            lax.dot_general(lhs[0], high, dims, preferred_element_type=F32)
            + lax.dot_general(lhs[0], low, dims, preferred_element_type=F32)
            + lax.dot_general(lhs[1], high, dims, preferred_element_type=F32)
        )

    multiply_arrivals(ring_in, project)

    rim = pltpu.make_async_remote_copy(
        src_ref=raw_ref.at[pl.ds(rows - RIM, RIM), pl.ds(0, width)],
        dst_ref=prior_ref,
        send_sem=rim_sem.at[0],
        recv_sem=rim_sem.at[1],
        device_id=after,
        device_id_type=MESH,
    )
    padded_ref[RIM:] = raw_ref[:, :width]
    rim.start()

    row_ids = lax.broadcasted_iota(jnp.int32, (CHUNK, CHUNK), 0)
    col_ids = lax.broadcasted_iota(jnp.int32, (CHUNK, CHUNK), 1)
    lower = row_ids >= col_ids
    strict = row_ids > col_ids
    apart = row_ids ^ col_ids
    identity = (row_ids == col_ids).astype(F32)
    ones_lower = lower.astype(BF16)
    ones_upper = (row_ids <= col_ids).astype(BF16)
    rate = rate_ref[0]
    mix = mixing_ref[...]
    weights = softplus(mix)
    mixing_ref[...] = weights
    betas = jax.nn.sigmoid(mix)
    taps = conv_ref[...]

    def prepare(c):
        base = c * CHUNK
        total = jnp.zeros((CHUNK, width), F32)
        for step in range(4):
            first = base + RIM - 3 + step
            total = total + taps[step:step + 1] * padded_ref[first:first + CHUNK]
        total = total * jax.nn.sigmoid(total)
        q, k, v = total[:, :DK], total[:, DK:2 * DK], total[:, 2 * DK:]
        q = q * lax.rsqrt(jnp.sum(q * q, axis=1, keepdims=True) + 1e-06)
        k = k * lax.rsqrt(jnp.sum(k * k, axis=1, keepdims=True) + 1e-06)
        beta = betas[base:base + CHUNK, 0:1]
        drop = jnp.broadcast_to(-rate * weights[base:base + CHUNK, 1:2], (CHUNK, CHUNK))
        high, low = split(drop)
        lowest = (drop - high.astype(F32) - low.astype(F32)).astype(BF16)
        sums = jnp.dot(ones_lower, jnp.concatenate([high, low, lowest], axis=1), preferred_element_type=F32)
        drift = sums[:, :CHUNK] + sums[:, CHUNK:2 * CHUNK] + sums[:, 2 * CHUNK:]
        docs = jnp.broadcast_to(doc_ref[c:c + 1].astype(F32), (CHUNK, CHUNK)).astype(BF16)
        count_t = jnp.dot(docs, ones_upper, preferred_element_type=F32)
        count = count_t.T
        gap = (drift - drift.T) - 20.0 * (count - count_t)
        decay = jnp.where(lower, jnp.exp(jnp.where(lower, gap, 0.0)), 0.0)
        begin = jnp.exp(drift - 20.0 * count)
        last = slice(CHUNK - 1, CHUNK)
        tail = jnp.exp((drift[last] - drift) - 20.0 * (count[last] - count))
        both = product(left(jnp.concatenate([k, q], axis=0)), right(k.T))
        return dict(
            q=q, k=k, gram=jnp.where(strict, beta * both[:CHUNK], 0.0), cross=jnp.where(lower, both[CHUNK:], 0.0),
            decay=decay, begin=begin, end=begin[last], tail=tail, weighted_k=beta * k, weighted_v=beta * v,
        )

    parts = [None] * chunks
    for c in range(1, chunks):
        parts[c] = prepare(c)
    rim.wait_recv()
    padded_ref[:RIM] = jnp.where(me == 0, 0.0, prior_ref[...])
    parts[0] = prepare(0)

    inverses = [identity - jnp.where(apart == 1, part["gram"], 0.0) for part in parts]
    size = 2
    while size < CHUNK:
        member = (apart >= size) & (apart < 2 * size)
        rights = [right(inverse) for inverse in inverses]
        firsts = [product(left(jnp.where(member, part["gram"], 0.0)), rights[c]) for c, part in enumerate(parts)]
        inverses = [inverse - product(left(inverse), right(firsts[c])) for c, inverse in enumerate(inverses)]
        size *= 2

    starts = []
    state = None
    for c, part in enumerate(parts):
        part["x"] = product(left(inverses[c]), right(part["weighted_k"]))
        part["y"] = product(left(part["decay"] * inverses[c]), right(part["weighted_v"]))
        ends_t = jnp.concatenate([part["x"], part["y"] * part["tail"]], axis=1).T
        ended = product(left(ends_t), right(part["k"]))
        pair = jnp.concatenate([part["end"] * (identity - ended[:DK]), ended[DK:]], axis=0)
        starts.append(state)
        state = pair if state is None else join(state, pair)
    pair_ref[...] = state
    held_z[place_z] = state

    def finish(c):
        part = parts[c]
        own = part["begin"] * (part["q"] - product(left(part["cross"]), right(part["x"])))
        near_part = product(left(part["decay"] * part["cross"]), right(part["y"]))
        if starts[c] is not None:
            own_left = left(own)
            near_part = near_part + product(own_left, right(starts[c][DK:].T))
            own = product(own_left, right(starts[c][:DK].T))
        base = c * CHUNK
        carried_ref[base:base + CHUNK] = own
        local_ref[base:base + CHUNK] = mixing_ref[base:base + CHUNK, 2:3] * near_part

    for index in range(PARTS):
        ring_z.begin(index)
    hops = 0
    for c in range(chunks):
        finish(c)
        if c >= 1 and hops < ring_z.half:
            hops += 1
            ring_z.arrive(hops)
    ring_z.run(hops + 1)

    group = reduce_ring(held_z, tree_z, count_z, True)
    group_ref[...] = group
    held_x[place_x] = group
    pair_rows = lax.broadcasted_iota(jnp.int32, (2 * DK, DK), 0)
    pair_cols = lax.broadcasted_iota(jnp.int32, (2 * DK, DK), 1)
    neutral = (pair_rows == pair_cols).astype(F32)
    states, carry = level_states(held_z, tree_z, count_z, place_z, neutral[:DK], neutral)
    for index in range(PARTS):
        ring_x.begin(index)
    done = len(states)

    def mixed(c, states, first):
        base = c * CHUNK
        carried = left(carried_ref[base:base + CHUNK])
        total = local_ref[base:base + CHUNK]
        for number, state in enumerate(states):
            column = first + number
            total = total + mixing_ref[base:base + CHUNK, column:column + 1] * product(carried, state)
        return total

    turned = [right(value.T) for value in states]
    for c in range(chunks):
        local_ref[c * CHUNK:(c + 1) * CHUNK] = mixed(c, turned, 3)
    ring_x.run()
    reduce_ring(held_x, tree_x, count_x, False)
    states, carry = level_states(held_x, tree_x, count_x, place_x, carry, neutral)
    turned = [right(value.T) for value in states]
    for c in range(chunks):
        total = mixed(c, turned, 3 + done)
        scale = lax.rsqrt(jnp.mean(total * total, axis=1, keepdims=True) + 1e-05)
        gate = raw_ref[c * CHUNK:(c + 1) * CHUNK, width:]
        normed = total * scale * gain_ref[...] * (gate * jax.nn.sigmoid(gate))
        normed_ref[c * CHUNK:(c + 1) * CHUNK] = normed
        held_out[head, c * CHUNK:(c + 1) * CHUNK] = normed
        if c >= 1:
            ring_out.begin(c - 1)
    ring_out.begin(chunks - 1)

    def combine(lhs, begin):
        high, low = split(w_out[pl.ds(begin, 2 * DK), :])
        both = jnp.concatenate([high, low], axis=1)
        out = jnp.dot(lhs[0], both, preferred_element_type=F32)
        out_ref[...] += out[:, :DK] + out[:, DK:] + jnp.dot(lhs[1], high, preferred_element_type=F32)

    multiply_arrivals(ring_out, combine)
    rim.wait_send()
    for ring in (ring_in, ring_z, ring_x, ring_out):
        ring.end()


def shards(tokens, w_proj, w_mix, conv_w, rates, doc_start, norm_gain, w_out):
    rows = tokens.shape[0]
    heads = lax.axis_size("head")
    count = lax.axis_size("ctx")
    count_z = min(NZ, count)
    count_x = count // count_z
    vmem = lambda *shape: pltpu.VMEM(shape, F32)
    sems = lambda *shape: pltpu.SemaphoreType.DMA(shape)
    pair = (2 * DK, DK)
    return pl.pallas_call(
        layer,
        out_shape=jax.ShapeDtypeStruct((rows, DK), F32),
        in_specs=[VMEM, ANY, VMEM, VMEM, SMEM, VMEM, VMEM, ANY],
        out_specs=VMEM,
        scratch_shapes=[
            vmem(heads, rows, DK), vmem(heads, rows, DK), vmem(*w_proj.shape), vmem(*w_out.shape),
            vmem(rows, 4 * DK), vmem(rows, w_mix.shape[1]), vmem(rows + RIM, 3 * DK), vmem(RIM, 3 * DK),
            vmem(*pair), vmem(count_z, *pair), vmem(count_z.bit_length() - 2, count_z // 2, *pair),
            vmem(*pair), vmem(count_x, *pair), vmem(max(count_x.bit_length() - 2, 1), count_x // 2, *pair),
            vmem(rows, DK), vmem(rows, DK), vmem(rows, DK),
            sems(2), sems(2), sems(2, 2, heads // 4, PARTS), sems(2, 2, heads // 4, PARTS),
            sems(2, heads // 2, PARTS), sems(2, heads // 2, PARTS),
            sems(2, count_z // 2, PARTS), sems(2, count_z // 2, PARTS),
            sems(2, count_x // 2, PARTS), sems(2, count_x // 2, PARTS),
        ],
        compiler_params=pltpu.CompilerParams(collective_id=0, has_side_effects=True, vmem_limit_bytes=56 << 20),
        name="layer",
    )(tokens, w_proj, w_mix.T, conv_w, rates, doc_start.reshape(-1, CHUNK), norm_gain[None, :], w_out)


def solution(mesh):
    placed = (
        P("ctx", "head"),
        P(None, "head"),
        P(None, "head"),
        P(None, "head"),
        P("head"),
        P("ctx"),
        P("head"),
        P(None, "head"),
    )
    return jax.shard_map(
        shards, mesh=mesh, in_specs=placed, out_specs=P("ctx", "head"), check_vma=False
    )
```

```python
import jax
import jax.numpy as jnp
from jax import lax
from jax.experimental import pallas as pl
from jax.experimental.pallas import tpu as pltpu
from jax.sharding import PartitionSpec as P

F32 = jnp.float32
BF16 = jnp.bfloat16
DK = 128
CHUNK = 128
RIM = 8
NZ = 16
PARTS_Y, PARTS_Z, PARTS_X = 4, 8, 4
MESH = pl.DeviceIdType.MESH
VMEM = pl.BlockSpec(memory_space=pltpu.VMEM)
SMEM = pl.BlockSpec(memory_space=pltpu.SMEM)
HBM = pl.BlockSpec(memory_space=pltpu.HBM)


def split(value):
    high = value.astype(BF16)
    return high, (value - high.astype(F32)).astype(BF16)


def left(value):
    high, low = split(value)
    return jnp.concatenate([high, low], axis=1)


def right(value):
    high, low = split(value)
    both = jnp.concatenate([high, low], axis=1)
    return jnp.concatenate([both, both], axis=0)


def product(lhs, rhs):
    out = jnp.dot(lhs, rhs, preferred_element_type=F32)
    return out[:, :DK] + out[:, DK:]


def softplus(value):
    return jnp.maximum(value, 0.0) + jnp.log1p(jnp.exp(-jnp.abs(value)))


def join(first, second):
    moved = product(left(first), right(second[:DK]))
    return jnp.concatenate([moved[:DK], moved[DK:] + second[DK:]], axis=0)


class Ring:
    def __init__(self, parts, place, n, targets, source, held, send_sem, recv_sem, stride=1, phase=0, pass_on=None):
        self.place, self.n, self.targets, self.source, self.held = place, n, targets, source, held
        self.send_sem, self.recv_sem, self.stride, self.phase = send_sem, recv_sem, stride, phase
        self.pass_on, self.parts = pass_on, parts
        self.half = n // 2
        self.part = source.shape[0] // parts

    def slot(self, place):
        return place * self.stride + self.phase

    def span(self, index):
        return pl.ds(index * self.part, self.part)

    def goes(self, direction, hop, index):
        longest = self.half if (index < self.parts // 2) == (direction == 0) else self.half - 1
        return hop <= longest

    def offset(self, direction, hop):
        return lax.rem(self.n - hop if direction == 0 else hop + 0, self.n)

    def copy(self, direction, hop, index, first=False):
        slot = self.slot(self.place if first else lax.rem(self.place + self.offset(direction, hop), self.n))
        source = self.source if first else self.held.at[slot]
        return pltpu.make_async_remote_copy(
            src_ref=source.at[self.span(index)],
            dst_ref=self.held.at[slot, self.span(index)],
            send_sem=self.send_sem.at[direction, hop, index],
            recv_sem=self.recv_sem.at[direction, hop, index],
            device_id=self.targets[direction],
            device_id_type=MESH,
        )

    def begin(self, index):
        for direction in range(2):
            if self.goes(direction, 1, index):
                self.copy(direction, 0, index, True).start()
        if self.pass_on is not None:
            self.pass_on(self.slot(self.place), 0, index, self.source).start()

    def arrive(self, hop, guard=True):
        for index in range(self.parts):
            for direction in range(2):
                here = guard & self.goes(direction, hop, index)

                @pl.when(here)
                def _():
                    self.copy(direction, hop - 1, index).wait_recv()

                @pl.when(guard & self.goes(direction, hop + 1, index))
                def _():
                    self.copy(direction, hop, index).start()

                if self.pass_on is not None:
                    @pl.when(here)
                    def _():
                        offset = self.offset(direction, hop)
                        slot = self.slot(lax.rem(self.place + offset, self.n))
                        self.pass_on(slot, offset, index, self.held.at[slot]).start()

    def run(self, first=1):
        def step(hop, carry):
            self.arrive(hop)
            return carry

        lax.fori_loop(first, self.half + 1, step, 0)

    def end(self):
        for index in range(self.parts):
            for direction in range(2):
                for hop in range(self.half):
                    if self.goes(direction, hop + 1, index):
                        self.copy(direction, hop, index, True).wait_send()
            if self.pass_on is not None:
                for offset in range(self.n):
                    self.pass_on(self.slot(self.place), offset, index, self.source).wait_send()


class PairRing:
    def __init__(self, parts, place, n, targets, source, held, send_sem, recv_sem):
        self.place, self.n, self.targets, self.source, self.held = place, n, targets, source, held
        self.send_sem, self.recv_sem, self.parts = send_sem, recv_sem, parts
        self.last = n // 2 - 1
        self.part = source.shape[0] // parts

    def copy(self, hop, index):
        rightward = lax.rem(self.place + hop, 2) == 1
        origin = lax.rem(self.place + jnp.where(rightward, self.n - hop, hop), self.n)
        slot = origin // 2
        direction = jnp.where(rightward, 0, 1)
        span = pl.ds(index * self.part, self.part)
        source = self.source if isinstance(hop, int) and hop == 0 else self.held.at[slot]
        return pltpu.make_async_remote_copy(
            src_ref=source.at[span],
            dst_ref=self.held.at[slot, span],
            send_sem=self.send_sem.at[direction, hop, index],
            recv_sem=self.recv_sem.at[direction, hop, index],
            device_id={"ctx": jnp.where(rightward, self.targets[0]["ctx"], self.targets[1]["ctx"])},
            device_id_type=MESH,
        )

    def begin(self):
        for index in range(self.parts):
            self.copy(0, index).start()

    def run(self):
        def step(hop, carry):
            for index in range(self.parts):
                origin = lax.rem(self.place + jnp.where(lax.rem(self.place + hop, 2) == 1, self.n - hop, hop), self.n)
                direction = jnp.where(lax.rem(self.place + hop, 2) == 1, 0, 1)
                span = pl.ds(index * self.part, self.part)
                slot = self.held.at[origin // 2, span]
                pltpu.make_async_remote_copy(
                    src_ref=slot,
                    dst_ref=slot,
                    send_sem=self.send_sem.at[direction, hop - 1, index],
                    recv_sem=self.recv_sem.at[direction, hop - 1, index],
                    device_id=self.targets[0],
                    device_id_type=MESH,
                ).wait_recv()

                @pl.when(hop < self.last)
                def _():
                    self.copy(hop, index).start()

            return carry

        lax.fori_loop(1, self.last + 1, step, 0)

    def end(self):
        for index in range(self.parts):
            for hop in range(self.last):
                self.copy(hop, index).wait_send()


def multiply_arrivals(ring, multiply):
    def step(hop, carry):
        ring.arrive(hop, hop >= 1)

        def block(which, inner):
            offset = lax.rem(jnp.where(which == 0, hop, ring.n - hop), ring.n)
            there = lax.rem(ring.place + offset, ring.n)
            for index in range(ring.parts):
                other = there * 2 + 1 - ring.phase
                ring.pass_on(other, offset, index, ring.held.at[other]).wait_recv()
            lhs = jnp.concatenate([ring.held[there * 2], ring.held[there * 2 + 1]], axis=1)
            multiply(split(lhs), pl.multiple_of(there * 2 * DK, 2 * DK))
            return inner

        lax.fori_loop(0, jnp.where((hop == 0) | (hop == ring.half), 1, 2), block, 0)
        return carry

    lax.fori_loop(0, ring.half + 1, step, 0)


def reduce_ring(held, tree, count, last):
    nodes = [held[index] for index in range(count)]
    level = 0
    while len(nodes) > (1 if last else 2):
        nodes = [join(nodes[2 * index], nodes[2 * index + 1]) for index in range(len(nodes) // 2)]
        if len(nodes) > 1:
            for index, node in enumerate(nodes):
                tree[level, index] = node
        level += 1
    return nodes[0]


def level_states(held, tree, count, place, carry, neutral):
    states = []
    for level in range(count.bit_length() - 1):
        upper = (place >> level) & 1 == 1
        index = jnp.maximum((place >> level) - 1, 0)
        node = held[index] if level == 0 else tree[level - 1, index]
        moved = product(left(jnp.where(upper, node, neutral)), right(carry))
        carry = moved[:DK]
        states.append(moved[DK:])
    return states, carry


def layer(tokens_ref, w_proj_ref, w_mix_hbm, conv_hbm, rate_ref, doc_hbm, gain_hbm, w_out_ref, out_ref,
          held_in, held_out, w_proj, w_out, w_mix_ref, conv_ref, doc_ref, gain_ref, raw_ref, mixing_ref, padded_ref, prior_ref,
          pair_ref, buddy_ref, near_pair_ref, held_z, tree_z, group_ref, held_x, tree_x, local_ref, carried_ref, normed_ref, kept_ref, start_ref,
          load_sem, rim_sem, buddy_sem, send_y, recv_y, near_send, near_recv,
          send_z, recv_z, send_x, recv_x):
    rows = tokens_ref.shape[0]
    chunks = rows // CHUNK
    width = 3 * DK
    heads = held_in.shape[0]
    chips = heads // 2
    count_z, count_x = 2 * held_z.shape[0], held_x.shape[0]
    blocks = count_z * count_x

    head = lax.axis_index("head")
    chip, core = head // 2, lax.rem(head, 2)
    me = lax.axis_index("ctx")
    place_x, place_z = me // count_z, lax.rem(me, count_z)
    targets_y = [{"head": lax.rem(chip + offset, chips) * 2 + core} for offset in (1, chips - 1)]
    sibling = {"head": head + 1 - 2 * core}
    targets_z = [
        {"ctx": place_x * count_z + lax.rem(place_z + offset, count_z)} for offset in (1, count_z - 1)
    ]
    targets_x = [
        {"ctx": lax.rem(place_x + offset, count_x) * count_z + place_z} for offset in (1, count_x - 1)
    ]
    after, before = {"ctx": lax.rem(me + 1, blocks)}, {"ctx": lax.rem(me + blocks - 1, blocks)}

    first_load = pltpu.make_async_copy(tokens_ref, held_in.at[head], load_sem.at[0])
    first_load.start()
    pairs = [(w_mix_hbm, w_mix_ref), (w_proj_ref, w_proj), (conv_hbm, conv_ref), (doc_hbm, doc_ref),
             (gain_hbm, gain_ref), (w_out_ref, w_out)]
    loads = [pltpu.make_async_copy(source, target, load_sem.at[1 + index])
             for index, (source, target) in enumerate(pairs)]
    for load in loads:
        load.start()
    barrier = pltpu.get_barrier_semaphore()
    partners = targets_y + [sibling] + targets_z + targets_x + [after, before]
    for partner in partners:
        pl.semaphore_signal(barrier, inc=1, device_id=partner, device_id_type=MESH)
    pl.semaphore_wait(barrier, len(partners))

    def near(held, number):
        def copy(slot, offset, index, source):
            part = rows // PARTS_Y
            span = pl.ds(index * part, part)
            return pltpu.make_async_remote_copy(
                src_ref=source.at[span],
                dst_ref=held.at[slot, span],
                send_sem=near_send.at[number, offset, index],
                recv_sem=near_recv.at[number, offset, index],
                device_id=sibling,
                device_id_type=MESH,
            )

        return copy

    ring_in = Ring(PARTS_Y, chip, chips, targets_y, held_in.at[head], held_in, send_y.at[0], recv_y.at[0], 2, core, near(held_in, 0))
    ring_out = Ring(PARTS_Y, chip, chips, targets_y, normed_ref, held_out, send_y.at[1], recv_y.at[1], 2, core, near(held_out, 1))
    ring_z = PairRing(PARTS_Z, place_z, count_z, targets_z, near_pair_ref, held_z, send_z, recv_z)
    odd = lax.rem(place_z, 2) == 1
    buddy = pltpu.make_async_remote_copy(
        src_ref=pair_ref,
        dst_ref=buddy_ref,
        send_sem=buddy_sem.at[0],
        recv_sem=buddy_sem.at[1],
        device_id={"ctx": me + jnp.where(odd, -1, 1)},
        device_id_type=MESH,
    )
    ring_x = Ring(PARTS_X, place_x, count_x, targets_x, group_ref, held_x, send_x, recv_x)

    first_load.wait()
    for index in range(PARTS_Y):
        ring_in.begin(index)
    raw_ref[...] = jnp.zeros_like(raw_ref)
    mixing_ref[...] = jnp.zeros_like(mixing_ref)
    out_ref[...] = jnp.zeros_like(out_ref)
    for load in loads:
        load.wait()

    def project(lhs, begin):
        high, low = split(w_proj[pl.ds(begin, 2 * DK), :])
        raw_ref[...] += (
            jnp.dot(lhs[0], high, preferred_element_type=F32)
            + jnp.dot(lhs[0], low, preferred_element_type=F32)
            + jnp.dot(lhs[1], high, preferred_element_type=F32)
        )
        high, low = split(w_mix_ref[:, pl.ds(begin, 2 * DK)])
        dims = (((1,), (1,)), ((), ()))
        mixing_ref[...] += (
            lax.dot_general(lhs[0], high, dims, preferred_element_type=F32)
            + lax.dot_general(lhs[0], low, dims, preferred_element_type=F32)
            + lax.dot_general(lhs[1], high, dims, preferred_element_type=F32)
        )

    multiply_arrivals(ring_in, project)

    rim = pltpu.make_async_remote_copy(
        src_ref=raw_ref.at[pl.ds(rows - RIM, RIM), pl.ds(0, width)],
        dst_ref=prior_ref,
        send_sem=rim_sem.at[0],
        recv_sem=rim_sem.at[1],
        device_id=after,
        device_id_type=MESH,
    )
    padded_ref[RIM:] = raw_ref[:, :width]
    rim.start()

    row_ids = lax.broadcasted_iota(jnp.int32, (CHUNK, CHUNK), 0)
    col_ids = lax.broadcasted_iota(jnp.int32, (CHUNK, CHUNK), 1)
    lower = row_ids >= col_ids
    strict = row_ids > col_ids
    apart = row_ids ^ col_ids
    identity = (row_ids == col_ids).astype(F32)
    ones_lower = lower.astype(BF16)
    ones_upper = (row_ids <= col_ids).astype(BF16)
    rate = rate_ref[0]
    mix = mixing_ref[...]
    weights = softplus(mix)
    mixing_ref[...] = weights
    betas = jax.nn.sigmoid(mix)

    def convolve(base, first_column, columns):
        total = jnp.zeros((CHUNK, columns), F32)
        span = pl.ds(first_column, columns)
        window = padded_ref[pl.ds(base, CHUNK + RIM), span]
        for step in range(4):
            first = RIM - 3 + step
            total = total + conv_ref[step:step + 1, span] * window[first:first + CHUNK]
        return total * jax.nn.sigmoid(total)

    def unit(value):
        return value * lax.rsqrt(jnp.sum(value * value, axis=1, keepdims=True) + 1e-06)

    def prepare(c):
        base = c * CHUNK
        both = convolve(base, DK, 2 * DK)
        k, v = unit(both[:, :DK]), both[:, DK:]
        beta = betas[base:base + CHUNK, 0:1]
        drop = jnp.broadcast_to(-rate * weights[base:base + CHUNK, 1:2], (CHUNK, CHUNK))
        high, low = split(drop)
        lowest = (drop - high.astype(F32) - low.astype(F32)).astype(BF16)
        sums = jnp.dot(ones_lower, jnp.concatenate([high, low, lowest], axis=1), preferred_element_type=F32)
        drift = sums[:, :CHUNK] + sums[:, CHUNK:2 * CHUNK] + sums[:, 2 * CHUNK:]
        docs = jnp.broadcast_to(doc_ref[c:c + 1].astype(F32), (CHUNK, CHUNK)).astype(BF16)
        count_t = jnp.dot(docs, ones_upper, preferred_element_type=F32)
        count = count_t.T
        gap = (drift - drift.T) - 20.0 * (count - count_t)
        decay = jnp.where(lower, jnp.exp(jnp.where(lower, gap, 0.0)), 0.0)
        begin = jnp.exp(drift - 20.0 * count)
        last = slice(CHUNK - 1, CHUNK)
        tail = jnp.exp((drift[last] - drift) - 20.0 * (count[last] - count))
        gram = jnp.where(strict, beta * product(left(k), right(k.T)), 0.0)
        kept_ref[c, 0] = k
        kept_ref[c, 1] = decay
        kept_ref[c, 2] = begin
        return dict(k=k, gram=gram, decay=decay, end=begin[last], tail=tail, weighted_k=beta * k, weighted_v=beta * v)

    parts = [None] * chunks
    for c in range(1, chunks):
        parts[c] = prepare(c)
    rim.wait_recv()
    padded_ref[:RIM] = jnp.where(me == 0, 0.0, prior_ref[...])
    parts[0] = prepare(0)

    inverses = [identity - jnp.where(apart == 1, part["gram"], 0.0) for part in parts]
    size = 2
    while size < CHUNK:
        member = (apart >= size) & (apart < 2 * size)
        rights = [right(inverse) for inverse in inverses]
        firsts = [product(left(jnp.where(member, part["gram"], 0.0)), rights[c]) for c, part in enumerate(parts)]
        inverses = [inverse - product(left(inverse), right(firsts[c])) for c, inverse in enumerate(inverses)]
        size *= 2

    pair_rows = lax.broadcasted_iota(jnp.int32, (2 * DK, DK), 0)
    pair_cols = lax.broadcasted_iota(jnp.int32, (2 * DK, DK), 1)
    neutral = (pair_rows == pair_cols).astype(F32)
    state = None
    for c, part in enumerate(parts):
        factor_x = product(left(inverses[c]), right(part["weighted_k"]))
        factor_y = product(left(part["decay"] * inverses[c]), right(part["weighted_v"]))
        kept_ref[c, 3] = factor_x
        kept_ref[c, 4] = factor_y
        ends_t = jnp.concatenate([factor_x, factor_y * part["tail"]], axis=1).T
        ended = product(left(ends_t), right(part["k"]))
        pair = jnp.concatenate([part["end"] * (identity - ended[:DK]), ended[DK:]], axis=0)
        start_ref[c] = neutral if state is None else state
        state = pair if state is None else join(state, pair)
    pair_ref[...] = state
    held_z[place_z // 2] = state
    buddy.start()

    def finish(c):
        base = pl.multiple_of(c * CHUNK, CHUNK)
        q = unit(convolve(base, 0, DK))
        k, decay, begin, factor_x, factor_y = [kept_ref[c, index] for index in range(5)]
        cross = jnp.where(lower, product(left(q), right(k.T)), 0.0)
        own = left(begin * (q - product(left(cross), right(factor_x))))
        near_part = product(left(decay * cross), right(factor_y))
        near_part = near_part + product(own, right(start_ref[c, DK:].T))
        span = pl.ds(base, CHUNK)
        carried_ref[span] = product(own, right(start_ref[c, :DK].T))
        local_ref[span] = mixing_ref[span, 2:3] * near_part

    def finish_step(c, carry):
        finish(c)
        return carry

    early = chunks - 1
    lax.fori_loop(0, early, finish_step, 0)
    buddy.wait_recv()
    mine, other = pair_ref[...], buddy_ref[...]
    near_pair = join(jnp.where(odd, other, mine), jnp.where(odd, mine, other))
    near_pair_ref[...] = near_pair
    held_z[place_z // 2] = near_pair
    ring_z.begin()
    lax.fori_loop(early, chunks, finish_step, 0)
    ring_z.run()

    group = reduce_ring(held_z, tree_z, count_z // 2, True)
    group_ref[...] = group
    held_x[place_x] = group
    for index in range(PARTS_X):
        ring_x.begin(index)
    nearest = jnp.where(odd, buddy_ref[...], neutral)
    states, carry = level_states(held_z, tree_z, count_z // 2, place_z // 2, nearest[:DK], neutral)
    states = [nearest[DK:]] + states
    done = len(states)

    def mixed(c, states, first):
        base = c * CHUNK
        carried = left(carried_ref[base:base + CHUNK])
        total = local_ref[base:base + CHUNK]
        for number, state in enumerate(states):
            column = first + number
            total = total + mixing_ref[base:base + CHUNK, column:column + 1] * product(carried, state)
        return total

    turned = [right(value.T) for value in states]
    for c in range(chunks):
        local_ref[c * CHUNK:(c + 1) * CHUNK] = mixed(c, turned, 3)
    ring_x.run()
    reduce_ring(held_x, tree_x, count_x, False)
    states, carry = level_states(held_x, tree_x, count_x, place_x, carry, neutral)
    turned = [right(value.T) for value in states]

    def send(c):
        for index in range(c * PARTS_Y // chunks, (c + 1) * PARTS_Y // chunks):
            ring_out.begin(index)

    for c in range(chunks):
        total = mixed(c, turned, 3 + done)
        scale = lax.rsqrt(jnp.mean(total * total, axis=1, keepdims=True) + 1e-05)
        gate = raw_ref[c * CHUNK:(c + 1) * CHUNK, width:]
        normed = total * scale * gain_ref[...] * (gate * jax.nn.sigmoid(gate))
        normed_ref[c * CHUNK:(c + 1) * CHUNK] = normed
        held_out[head, c * CHUNK:(c + 1) * CHUNK] = normed
        if c >= 1:
            send(c - 1)
    send(chunks - 1)

    def combine(lhs, begin):
        high, low = split(w_out[pl.ds(begin, 2 * DK), :])
        both = jnp.concatenate([high, low], axis=1)
        out = jnp.dot(lhs[0], both, preferred_element_type=F32)
        out_ref[...] += out[:, :DK] + out[:, DK:] + jnp.dot(lhs[1], high, preferred_element_type=F32)

    multiply_arrivals(ring_out, combine)
    rim.wait_send()
    buddy.wait_send()
    for ring in (ring_in, ring_z, ring_x, ring_out):
        ring.end()


def shards(tokens, w_proj, w_mix, conv_w, rates, doc_start, norm_gain, w_out):
    rows = tokens.shape[0]
    heads = lax.axis_size("head")
    count = lax.axis_size("ctx")
    count_z = min(NZ, count)
    count_x = count // count_z
    vmem = lambda *shape: pltpu.VMEM(shape, F32)
    sems = lambda *shape: pltpu.SemaphoreType.DMA(shape)
    pair = (2 * DK, DK)
    return pl.pallas_call(
        layer,
        out_shape=jax.ShapeDtypeStruct((rows, DK), F32),
        in_specs=[HBM, HBM, HBM, HBM, SMEM, HBM, HBM, HBM],
        out_specs=VMEM,
        scratch_shapes=[
            vmem(heads, rows, DK), vmem(heads, rows, DK), vmem(*w_proj.shape), vmem(*w_out.shape),
            vmem(w_mix.shape[1], w_mix.shape[0]), vmem(*conv_w.shape),
            pltpu.VMEM((rows // CHUNK, CHUNK), jnp.int32), vmem(1, DK),
            vmem(rows, 4 * DK), vmem(rows, w_mix.shape[1]), vmem(rows + RIM, 3 * DK), vmem(RIM, 3 * DK),
            vmem(*pair), vmem(*pair), vmem(*pair), vmem(count_z // 2, *pair),
            vmem(max(count_z.bit_length() - 3, 1), max(count_z // 4, 1), *pair),
            vmem(*pair), vmem(count_x, *pair), vmem(max(count_x.bit_length() - 2, 1), count_x // 2, *pair),
            vmem(rows, DK), vmem(rows, DK), vmem(rows, DK), vmem(rows // CHUNK, 5, CHUNK, CHUNK), vmem(rows // CHUNK, *pair),
            sems(7), sems(2), sems(2), sems(2, 2, heads // 4, PARTS_Y), sems(2, 2, heads // 4, PARTS_Y),
            sems(2, heads // 2, PARTS_Y), sems(2, heads // 2, PARTS_Y),
            sems(2, count_z // 2, PARTS_Z), sems(2, count_z // 2, PARTS_Z),
            sems(2, count_x // 2, PARTS_X), sems(2, count_x // 2, PARTS_X),
        ],
        compiler_params=pltpu.CompilerParams(collective_id=0, has_side_effects=True, vmem_limit_bytes=56 << 20),
        name="layer",
    )(tokens, w_proj, w_mix.T, conv_w, rates, doc_start.reshape(-1, CHUNK), norm_gain[None, :], w_out)


def solution(mesh):
    placed = (
        P("ctx", "head"),
        P(None, "head"),
        P(None, "head"),
        P(None, "head"),
        P("head"),
        P("ctx"),
        P("head"),
        P(None, "head"),
    )
    return jax.shard_map(
        shards, mesh=mesh, in_specs=placed, out_specs=P("ctx", "head"), check_vma=False
    )
```

```python
import jax
import jax.numpy as jnp
from jax import lax
from jax.experimental import pallas as pl
from jax.experimental.pallas import tpu as pltpu
from jax.sharding import PartitionSpec as P

F32 = jnp.float32
BF16 = jnp.bfloat16
DK = 128
CHUNK = 128
RIM = 8
NZ = 16
PARTS_Y, PARTS_Z, PARTS_X = 4, 4, 4
MESH = pl.DeviceIdType.MESH
VMEM = pl.BlockSpec(memory_space=pltpu.VMEM)
SMEM = pl.BlockSpec(memory_space=pltpu.SMEM)
HBM = pl.BlockSpec(memory_space=pltpu.HBM)


def split(value):
    high = value.astype(BF16)
    return high, (value - high.astype(F32)).astype(BF16)


def left(value):
    high, low = split(value)
    return jnp.concatenate([high, low], axis=1)


def right(value):
    high, low = split(value)
    both = jnp.concatenate([high, low], axis=1)
    return jnp.concatenate([both, both], axis=0)


def product(lhs, rhs):
    out = jnp.dot(lhs, rhs, preferred_element_type=F32)
    return out[:, :DK] + out[:, DK:]


def softplus(value):
    return jnp.maximum(value, 0.0) + jnp.log1p(jnp.exp(-jnp.abs(value)))


def join(first, second):
    moved = product(left(first), right(second[:DK]))
    return jnp.concatenate([moved[:DK], moved[DK:] + second[DK:]], axis=0)


class Ring:
    def __init__(self, parts, place, n, targets, source, held, send_sem, recv_sem, stride=1, phase=0, pass_on=None):
        self.place, self.n, self.targets, self.source, self.held = place, n, targets, source, held
        self.send_sem, self.recv_sem, self.stride, self.phase = send_sem, recv_sem, stride, phase
        self.pass_on, self.parts = pass_on, parts
        self.half = n // 2
        self.part = source.shape[0] // parts

    def slot(self, place):
        return place * self.stride + self.phase

    def span(self, index):
        return pl.ds(index * self.part, self.part)

    def goes(self, direction, hop, index):
        longest = self.half if (index < self.parts // 2) == (direction == 0) else self.half - 1
        return hop <= longest

    def offset(self, direction, hop):
        return lax.rem(self.n - hop if direction == 0 else hop + 0, self.n)

    def copy(self, direction, hop, index, first=False):
        slot = self.slot(self.place if first else lax.rem(self.place + self.offset(direction, hop), self.n))
        source = self.source if first else self.held.at[slot]
        return pltpu.make_async_remote_copy(
            src_ref=source.at[self.span(index)],
            dst_ref=self.held.at[slot, self.span(index)],
            send_sem=self.send_sem.at[direction, hop, index],
            recv_sem=self.recv_sem.at[direction, hop, index],
            device_id=self.targets[direction],
            device_id_type=MESH,
        )

    def begin(self, index):
        for direction in range(2):
            if self.goes(direction, 1, index):
                self.copy(direction, 0, index, True).start()
        if self.pass_on is not None:
            self.pass_on(self.slot(self.place), 0, index, self.source).start()

    def arrive(self, hop, guard=True):
        for index in range(self.parts):
            for direction in range(2):
                here = guard & self.goes(direction, hop, index)

                @pl.when(here)
                def _():
                    self.copy(direction, hop - 1, index).wait_recv()

                @pl.when(guard & self.goes(direction, hop + 1, index))
                def _():
                    self.copy(direction, hop, index).start()

                if self.pass_on is not None:
                    @pl.when(here)
                    def _():
                        offset = self.offset(direction, hop)
                        slot = self.slot(lax.rem(self.place + offset, self.n))
                        self.pass_on(slot, offset, index, self.held.at[slot]).start()

    def run(self, first=1):
        def step(hop, carry):
            self.arrive(hop)
            return carry

        lax.fori_loop(first, self.half + 1, step, 0)

    def end(self):
        for index in range(self.parts):
            for direction in range(2):
                for hop in range(self.half):
                    if self.goes(direction, hop + 1, index):
                        self.copy(direction, hop, index, True).wait_send()
            if self.pass_on is not None:
                for offset in range(self.n):
                    self.pass_on(self.slot(self.place), offset, index, self.source).wait_send()


class PairRing:
    def __init__(self, parts, place, n, targets, source, held, send_sem, recv_sem):
        self.place, self.n, self.targets, self.source, self.held = place, n, targets, source, held
        self.send_sem, self.recv_sem, self.parts = send_sem, recv_sem, parts
        self.last = n // 2 - 1
        self.part = source.shape[0] // parts

    def copy(self, hop, index):
        rightward = lax.rem(self.place + hop, 2) == 1
        origin = lax.rem(self.place + jnp.where(rightward, self.n - hop, hop), self.n)
        slot = origin // 2
        direction = jnp.where(rightward, 0, 1)
        span = pl.ds(index * self.part, self.part)
        source = self.source if isinstance(hop, int) and hop == 0 else self.held.at[slot]
        return pltpu.make_async_remote_copy(
            src_ref=source.at[span],
            dst_ref=self.held.at[slot, span],
            send_sem=self.send_sem.at[direction, hop, index],
            recv_sem=self.recv_sem.at[direction, hop, index],
            device_id={"ctx": jnp.where(rightward, self.targets[0]["ctx"], self.targets[1]["ctx"])},
            device_id_type=MESH,
        )

    def begin(self):
        for index in range(self.parts):
            self.copy(0, index).start()

    def run(self):
        def step(hop, carry):
            for index in range(self.parts):
                origin = lax.rem(self.place + jnp.where(lax.rem(self.place + hop, 2) == 1, self.n - hop, hop), self.n)
                direction = jnp.where(lax.rem(self.place + hop, 2) == 1, 0, 1)
                span = pl.ds(index * self.part, self.part)
                slot = self.held.at[origin // 2, span]
                pltpu.make_async_remote_copy(
                    src_ref=slot,
                    dst_ref=slot,
                    send_sem=self.send_sem.at[direction, hop - 1, index],
                    recv_sem=self.recv_sem.at[direction, hop - 1, index],
                    device_id=self.targets[0],
                    device_id_type=MESH,
                ).wait_recv()

                @pl.when(hop < self.last)
                def _():
                    self.copy(hop, index).start()

            return carry

        lax.fori_loop(1, self.last + 1, step, 0)

    def end(self):
        for index in range(self.parts):
            for hop in range(self.last):
                self.copy(hop, index).wait_send()


def multiply_arrivals(ring, multiply):
    def step(hop, carry):
        ring.arrive(hop, hop >= 1)

        def block(which, inner):
            offset = lax.rem(jnp.where(which == 0, hop, ring.n - hop), ring.n)
            there = lax.rem(ring.place + offset, ring.n)
            for index in range(ring.parts):
                other = there * 2 + 1 - ring.phase
                ring.pass_on(other, offset, index, ring.held.at[other]).wait_recv()
            lhs = jnp.concatenate([ring.held[there * 2], ring.held[there * 2 + 1]], axis=1)
            multiply(split(lhs), pl.multiple_of(there * 2 * DK, 2 * DK))
            return inner

        lax.fori_loop(0, jnp.where((hop == 0) | (hop == ring.half), 1, 2), block, 0)
        return carry

    lax.fori_loop(0, ring.half + 1, step, 0)


def reduce_ring(held, tree, count, last):
    nodes = [held[index] for index in range(count)]
    level = 0
    while len(nodes) > (1 if last else 2):
        nodes = [join(nodes[2 * index], nodes[2 * index + 1]) for index in range(len(nodes) // 2)]
        if len(nodes) > 1:
            for index, node in enumerate(nodes):
                tree[level, index] = node
        level += 1
    return nodes[0]


def level_states(held, tree, count, place, carry, neutral):
    states = []
    for level in range(count.bit_length() - 1):
        upper = (place >> level) & 1 == 1
        index = jnp.maximum((place >> level) - 1, 0)
        node = held[index] if level == 0 else tree[level - 1, index]
        moved = product(left(jnp.where(upper, node, neutral)), right(carry))
        carry = moved[:DK]
        states.append(moved[DK:])
    return states, carry


def layer(tokens_ref, w_proj_ref, w_mix_hbm, conv_hbm, rate_ref, doc_hbm, gain_hbm, w_out_ref, out_ref,
          held_in, held_out, w_proj, w_out, w_mix_ref, conv_ref, doc_ref, gain_ref, raw_ref, mixing_ref, padded_ref, prior_ref,
          pair_ref, buddy_ref, near_pair_ref, held_z, tree_z, group_ref, held_x, tree_x, local_ref, carried_ref, normed_ref, kept_ref, start_ref,
          load_sem, rim_sem, buddy_sem, send_y, recv_y, near_send, near_recv,
          send_z, recv_z, send_x, recv_x):
    rows = tokens_ref.shape[0]
    chunks = rows // CHUNK
    width = 3 * DK
    heads = held_in.shape[0]
    chips = heads // 2
    count_z, count_x = 2 * held_z.shape[0], held_x.shape[0]
    blocks = count_z * count_x

    head = lax.axis_index("head")
    chip, core = head // 2, lax.rem(head, 2)
    me = lax.axis_index("ctx")
    place_x, place_z = me // count_z, lax.rem(me, count_z)
    targets_y = [{"head": lax.rem(chip + offset, chips) * 2 + core} for offset in (1, chips - 1)]
    sibling = {"head": head + 1 - 2 * core}
    targets_z = [
        {"ctx": place_x * count_z + lax.rem(place_z + offset, count_z)} for offset in (1, count_z - 1)
    ]
    targets_x = [
        {"ctx": lax.rem(place_x + offset, count_x) * count_z + place_z} for offset in (1, count_x - 1)
    ]
    after, before = {"ctx": lax.rem(me + 1, blocks)}, {"ctx": lax.rem(me + blocks - 1, blocks)}

    first_load = pltpu.make_async_copy(tokens_ref, held_in.at[head], load_sem.at[0])
    first_load.start()
    pairs = [(w_mix_hbm, w_mix_ref), (w_proj_ref, w_proj), (conv_hbm, conv_ref), (doc_hbm, doc_ref),
             (gain_hbm, gain_ref), (w_out_ref, w_out)]
    loads = [pltpu.make_async_copy(source, target, load_sem.at[1 + index])
             for index, (source, target) in enumerate(pairs)]
    for load in loads:
        load.start()
    barrier = pltpu.get_barrier_semaphore()
    partners = targets_y + [sibling] + targets_z + targets_x + [after, before]
    for partner in partners:
        pl.semaphore_signal(barrier, inc=1, device_id=partner, device_id_type=MESH)
    pl.semaphore_wait(barrier, len(partners))

    def near(held, number):
        def copy(slot, offset, index, source):
            part = rows // PARTS_Y
            span = pl.ds(index * part, part)
            return pltpu.make_async_remote_copy(
                src_ref=source.at[span],
                dst_ref=held.at[slot, span],
                send_sem=near_send.at[number, offset, index],
                recv_sem=near_recv.at[number, offset, index],
                device_id=sibling,
                device_id_type=MESH,
            )

        return copy

    ring_in = Ring(PARTS_Y, chip, chips, targets_y, held_in.at[head], held_in, send_y.at[0], recv_y.at[0], 2, core, near(held_in, 0))
    ring_out = Ring(PARTS_Y, chip, chips, targets_y, normed_ref, held_out, send_y.at[1], recv_y.at[1], 2, core, near(held_out, 1))
    ring_z = PairRing(PARTS_Z, place_z, count_z, targets_z, near_pair_ref, held_z, send_z, recv_z)
    odd = lax.rem(place_z, 2) == 1
    buddy = pltpu.make_async_remote_copy(
        src_ref=pair_ref,
        dst_ref=buddy_ref,
        send_sem=buddy_sem.at[0],
        recv_sem=buddy_sem.at[1],
        device_id={"ctx": me + jnp.where(odd, -1, 1)},
        device_id_type=MESH,
    )
    ring_x = Ring(PARTS_X, place_x, count_x, targets_x, group_ref, held_x, send_x, recv_x)

    first_load.wait()
    for index in range(PARTS_Y):
        ring_in.begin(index)
    raw_ref[...] = jnp.zeros_like(raw_ref)
    mixing_ref[...] = jnp.zeros_like(mixing_ref)
    out_ref[...] = jnp.zeros_like(out_ref)
    for load in loads:
        load.wait()

    def project(lhs, begin):
        high, low = split(w_proj[pl.ds(begin, 2 * DK), :])
        raw_ref[...] += (
            jnp.dot(lhs[0], high, preferred_element_type=F32)
            + jnp.dot(lhs[0], low, preferred_element_type=F32)
            + jnp.dot(lhs[1], high, preferred_element_type=F32)
        )
        high, low = split(w_mix_ref[:, pl.ds(begin, 2 * DK)])
        dims = (((1,), (1,)), ((), ()))
        mixing_ref[...] += (
            lax.dot_general(lhs[0], high, dims, preferred_element_type=F32)
            + lax.dot_general(lhs[0], low, dims, preferred_element_type=F32)
            + lax.dot_general(lhs[1], high, dims, preferred_element_type=F32)
        )

    multiply_arrivals(ring_in, project)

    rim = pltpu.make_async_remote_copy(
        src_ref=raw_ref.at[pl.ds(rows - RIM, RIM), pl.ds(0, width)],
        dst_ref=prior_ref,
        send_sem=rim_sem.at[0],
        recv_sem=rim_sem.at[1],
        device_id=after,
        device_id_type=MESH,
    )
    padded_ref[RIM:] = raw_ref[:, :width]
    rim.start()

    row_ids = lax.broadcasted_iota(jnp.int32, (CHUNK, CHUNK), 0)
    col_ids = lax.broadcasted_iota(jnp.int32, (CHUNK, CHUNK), 1)
    lower = row_ids >= col_ids
    strict = row_ids > col_ids
    apart = row_ids ^ col_ids
    identity = (row_ids == col_ids).astype(F32)
    ones_lower = lower.astype(BF16)
    ones_upper = (row_ids <= col_ids).astype(BF16)
    rate = rate_ref[0]
    mix = mixing_ref[...]
    weights = softplus(mix)
    mixing_ref[...] = weights
    betas = jax.nn.sigmoid(mix)

    def convolve(base, first_column, columns):
        total = jnp.zeros((CHUNK, columns), F32)
        span = pl.ds(first_column, columns)
        window = padded_ref[pl.ds(base, CHUNK + RIM), span]
        for step in range(4):
            first = RIM - 3 + step
            total = total + conv_ref[step:step + 1, span] * window[first:first + CHUNK]
        return total * jax.nn.sigmoid(total)

    def unit(value):
        return value * lax.rsqrt(jnp.sum(value * value, axis=1, keepdims=True) + 1e-06)

    def prepare(c):
        base = c * CHUNK
        both = convolve(base, DK, 2 * DK)
        k, v = unit(both[:, :DK]), both[:, DK:]
        beta = betas[base:base + CHUNK, 0:1]
        drop = jnp.broadcast_to(-rate * weights[base:base + CHUNK, 1:2], (CHUNK, CHUNK))
        high, low = split(drop)
        lowest = (drop - high.astype(F32) - low.astype(F32)).astype(BF16)
        sums = jnp.dot(ones_lower, jnp.concatenate([high, low, lowest], axis=1), preferred_element_type=F32)
        drift = sums[:, :CHUNK] + sums[:, CHUNK:2 * CHUNK] + sums[:, 2 * CHUNK:]
        docs = jnp.broadcast_to(doc_ref[c:c + 1].astype(F32), (CHUNK, CHUNK)).astype(BF16)
        count_t = jnp.dot(docs, ones_upper, preferred_element_type=F32)
        count = count_t.T
        gap = (drift - drift.T) - 20.0 * (count - count_t)
        decay = jnp.where(lower, jnp.exp(jnp.where(lower, gap, 0.0)), 0.0)
        begin = jnp.exp(drift - 20.0 * count)
        last = slice(CHUNK - 1, CHUNK)
        tail = jnp.exp((drift[last] - drift) - 20.0 * (count[last] - count))
        gram = jnp.where(strict, beta * product(left(k), right(k.T)), 0.0)
        kept_ref[c, 0] = k
        kept_ref[c, 1] = decay
        kept_ref[c, 2] = begin
        return dict(k=k, gram=gram, decay=decay, end=begin[last], tail=tail, weighted_k=beta * k, weighted_v=beta * v)

    parts = [None] * chunks
    for c in range(1, chunks):
        parts[c] = prepare(c)
    rim.wait_recv()
    padded_ref[:RIM] = jnp.where(me == 0, 0.0, prior_ref[...])
    parts[0] = prepare(0)

    inverses = [identity - jnp.where(apart == 1, part["gram"], 0.0) for part in parts]
    size = 2
    while size < CHUNK:
        member = (apart >= size) & (apart < 2 * size)
        rights = [right(inverse) for inverse in inverses]
        firsts = [product(left(jnp.where(member, part["gram"], 0.0)), rights[c]) for c, part in enumerate(parts)]
        inverses = [inverse - product(left(inverse), right(firsts[c])) for c, inverse in enumerate(inverses)]
        size *= 2

    pair_rows = lax.broadcasted_iota(jnp.int32, (2 * DK, DK), 0)
    pair_cols = lax.broadcasted_iota(jnp.int32, (2 * DK, DK), 1)
    neutral = (pair_rows == pair_cols).astype(F32)
    state = None
    for c, part in enumerate(parts):
        factor_x = product(left(inverses[c]), right(part["weighted_k"]))
        factor_y = product(left(part["decay"] * inverses[c]), right(part["weighted_v"]))
        kept_ref[c, 3] = factor_x
        kept_ref[c, 4] = factor_y
        ends_t = jnp.concatenate([factor_x, factor_y * part["tail"]], axis=1).T
        ended = product(left(ends_t), right(part["k"]))
        pair = jnp.concatenate([part["end"] * (identity - ended[:DK]), ended[DK:]], axis=0)
        start_ref[c] = neutral if state is None else state
        state = pair if state is None else join(state, pair)
    pair_ref[...] = state
    held_z[place_z // 2] = state
    buddy.start()

    def finish(c):
        base = pl.multiple_of(c * CHUNK, CHUNK)
        q = unit(convolve(base, 0, DK))
        k, decay, begin, factor_x, factor_y = [kept_ref[c, index] for index in range(5)]
        cross = jnp.where(lower, product(left(q), right(k.T)), 0.0)
        own = left(begin * (q - product(left(cross), right(factor_x))))
        near_part = product(left(decay * cross), right(factor_y))
        near_part = near_part + product(own, right(start_ref[c, DK:].T))
        span = pl.ds(base, CHUNK)
        carried_ref[span] = product(own, right(start_ref[c, :DK].T))
        local_ref[span] = mixing_ref[span, 2:3] * near_part

    def finish_step(c, carry):
        finish(c)
        return carry

    early = chunks - 1
    lax.fori_loop(0, early, finish_step, 0)
    buddy.wait_recv()
    mine, other = pair_ref[...], buddy_ref[...]
    near_pair = join(jnp.where(odd, other, mine), jnp.where(odd, mine, other))
    near_pair_ref[...] = near_pair
    held_z[place_z // 2] = near_pair
    ring_z.begin()
    lax.fori_loop(early, chunks, finish_step, 0)
    ring_z.run()

    group = reduce_ring(held_z, tree_z, count_z // 2, True)
    group_ref[...] = group
    held_x[place_x] = group
    for index in range(PARTS_X):
        ring_x.begin(index)
    nearest = jnp.where(odd, buddy_ref[...], neutral)
    states, carry = level_states(held_z, tree_z, count_z // 2, place_z // 2, nearest[:DK], neutral)
    states = [nearest[DK:]] + states
    done = len(states)

    def mixed(c, states, first):
        base = c * CHUNK
        carried = left(carried_ref[base:base + CHUNK])
        total = local_ref[base:base + CHUNK]
        for number, state in enumerate(states):
            column = first + number
            total = total + mixing_ref[base:base + CHUNK, column:column + 1] * product(carried, state)
        return total

    turned = [right(value.T) for value in states]
    for c in range(chunks):
        local_ref[c * CHUNK:(c + 1) * CHUNK] = mixed(c, turned, 3)
    ring_x.run()
    reduce_ring(held_x, tree_x, count_x, False)
    states, carry = level_states(held_x, tree_x, count_x, place_x, carry, neutral)
    turned = [right(value.T) for value in states]

    def send(c):
        for index in range(c * PARTS_Y // chunks, (c + 1) * PARTS_Y // chunks):
            ring_out.begin(index)

    for c in range(chunks):
        total = mixed(c, turned, 3 + done)
        scale = lax.rsqrt(jnp.mean(total * total, axis=1, keepdims=True) + 1e-05)
        gate = raw_ref[c * CHUNK:(c + 1) * CHUNK, width:]
        normed = total * scale * gain_ref[...] * (gate * jax.nn.sigmoid(gate))
        normed_ref[c * CHUNK:(c + 1) * CHUNK] = normed
        held_out[head, c * CHUNK:(c + 1) * CHUNK] = normed
        if c >= 1:
            send(c - 1)
    send(chunks - 1)

    def combine(lhs, begin):
        high, low = split(w_out[pl.ds(begin, 2 * DK), :])
        both = jnp.concatenate([high, low], axis=1)
        out = jnp.dot(lhs[0], both, preferred_element_type=F32)
        out_ref[...] += out[:, :DK] + out[:, DK:] + jnp.dot(lhs[1], high, preferred_element_type=F32)

    multiply_arrivals(ring_out, combine)
    rim.wait_send()
    buddy.wait_send()
    for ring in (ring_in, ring_z, ring_x, ring_out):
        ring.end()


def shards(tokens, w_proj, w_mix, conv_w, rates, doc_start, norm_gain, w_out):
    rows = tokens.shape[0]
    heads = lax.axis_size("head")
    count = lax.axis_size("ctx")
    count_z = min(NZ, count)
    count_x = count // count_z
    vmem = lambda *shape: pltpu.VMEM(shape, F32)
    sems = lambda *shape: pltpu.SemaphoreType.DMA(shape)
    pair = (2 * DK, DK)
    return pl.pallas_call(
        layer,
        out_shape=jax.ShapeDtypeStruct((rows, DK), F32),
        in_specs=[HBM, HBM, HBM, HBM, SMEM, HBM, HBM, HBM],
        out_specs=VMEM,
        scratch_shapes=[
            vmem(heads, rows, DK), vmem(heads, rows, DK), vmem(*w_proj.shape), vmem(*w_out.shape),
            vmem(w_mix.shape[1], w_mix.shape[0]), vmem(*conv_w.shape),
            pltpu.VMEM((rows // CHUNK, CHUNK), jnp.int32), vmem(1, DK),
            vmem(rows, 4 * DK), vmem(rows, w_mix.shape[1]), vmem(rows + RIM, 3 * DK), vmem(RIM, 3 * DK),
            vmem(*pair), vmem(*pair), vmem(*pair), vmem(count_z // 2, *pair),
            vmem(max(count_z.bit_length() - 3, 1), max(count_z // 4, 1), *pair),
            vmem(*pair), vmem(count_x, *pair), vmem(max(count_x.bit_length() - 2, 1), count_x // 2, *pair),
            vmem(rows, DK), vmem(rows, DK), vmem(rows, DK), vmem(rows // CHUNK, 5, CHUNK, CHUNK), vmem(rows // CHUNK, *pair),
            sems(7), sems(2), sems(2), sems(2, 2, heads // 4, PARTS_Y), sems(2, 2, heads // 4, PARTS_Y),
            sems(2, heads // 2, PARTS_Y), sems(2, heads // 2, PARTS_Y),
            sems(2, count_z // 2, PARTS_Z), sems(2, count_z // 2, PARTS_Z),
            sems(2, count_x // 2, PARTS_X), sems(2, count_x // 2, PARTS_X),
        ],
        compiler_params=pltpu.CompilerParams(collective_id=0, has_side_effects=True, vmem_limit_bytes=56 << 20),
        name="layer",
    )(tokens, w_proj, w_mix.T, conv_w, rates, doc_start.reshape(-1, CHUNK), norm_gain[None, :], w_out)


def solution(mesh):
    placed = (
        P("ctx", "head"),
        P(None, "head"),
        P(None, "head"),
        P(None, "head"),
        P("head"),
        P("ctx"),
        P("head"),
        P(None, "head"),
    )
    return jax.shard_map(
        shards, mesh=mesh, in_specs=placed, out_specs=P("ctx", "head"), check_vma=False
    )
```
